256 devices in a mesh: gx: 8 (over z_lo, x), gy: 32 (over z_hi, y, core).
Axes of the slice: x: 4, y: 4, z: 8 (z_hi: 4, z_lo: 2; z = z_hi * 2 + z_lo), core: 2. Of those that a mesh axis runs over, the one named last changes fastest.
Arguments:
- node_feats: bfloat16 [65536, 512], P(('gx', 'gy')), may hold values from -24 to 24
- grad_out: bfloat16 [65536, 512], P(('gx', 'gy')), may hold values from -24 to 24
- log_sum_exp: float32 [8, 65536], P(None, ('gx', 'gy')), may hold values from 7.5 to 9
- w_query: bfloat16 [512, 512], replicated, may hold values from -0.25 to 0.25
- w_key: bfloat16 [512, 512], replicated, may hold values from -0.25 to 0.25
- w_value: bfloat16 [512, 512], replicated, may hold values from -0.25 to 0.25
- w_output: bfloat16 [512, 512], replicated, may hold values from -0.25 to 0.25
- partners: int32 [256, 3], replicated, may hold values from 0 to 255, as said below
Outputs:
- grad_nodes: bfloat16 [65536, 512], P(('gx', 'gy'))
- weight_grads: float32 [512, 2048], P('gx', 'gy')
The draws below stay inside these ranges and needn't reach their ends.
Inputs may be any that keep to these rules, and one draw needn't show every extreme that they name: Row b holds three different blocks, none of them b, and partners[partners[b, j], j] = b for each column j: each column is a perfect matching of the 256 blocks.
All inputs are finite; a program needn't handle non-finite values.
Results may differ from the reference program's by a relative error of at most 0.019.
Values may be sent and summed in bfloat16 or wider, within the bound.
A program may use at most 64 MiB of HBM per device.

```python
import jax
import jax.numpy as jnp
from jax import lax

D = 512
H = 8
HD = 64
BLOCK = 256
NB = 256
NODES = 65536


def draw_partners(key, part):
    first, second = jax.random.split(jax.random.fold_in(key, 11))
    order = jax.random.permutation(first, NB).astype(jnp.int32)
    masks = (jax.random.permutation(second, NB - 1)[:3] + 1).astype(jnp.int32)
    inverse = jnp.argsort(order).astype(jnp.int32)
    spots = jnp.bitwise_xor(inverse[:, None], masks[None, :])
    return order[spots].astype(jnp.int32)


def spiked(values, key, source, target, shards_of, factor):
    owner, partner = [(jnp.arange(values.shape[position]) // (values.shape[position] // shards_of)).reshape([-1 if axis == position else 1 for axis in range(values.ndim)]) for position in (source, target)]
    chosen = jax.random.permutation(key, shards_of)[partner]
    strong = (owner == chosen) | (owner == (partner + shards_of // 2) % shards_of)
    return jnp.where(strong, factor * values, values)


def level_of(stream_key, extent, pieces, low, high):
    gain = 1.0
    for position, shards_of in pieces:
        draws = jax.random.uniform(jax.random.fold_in(jax.random.fold_in(stream_key, 6), position), (shards_of,), jnp.float32, low / len(pieces), high / len(pieces))
        gain = gain * jnp.repeat(jnp.exp(draws), extent[position] // shards_of).reshape((-1,) + (1,) * (len(extent) - 1 - position))
    return gain


def noise(stream_key, dims, scale, bound, cuts=(), kind=jnp.bfloat16):
    drawn = jax.random.normal(stream_key, dims, jnp.float32) * scale
    if len(cuts) > 0:
        drawn = level_of(stream_key, dims, cuts, -0.22, 0.18) * drawn
    return jnp.clip(drawn, min=-bound, max=bound).astype(kind)


def gaussian_with(key, extent, width, most, pieces, heavy, held_as=jnp.bfloat16):
    result = width * jax.random.normal(key, extent, jnp.float32)
    if pieces:
        result = result * level_of(key, extent, pieces, -0.22, 0.18)
    return jnp.clip(spiked(result, jax.random.fold_in(key, 3), *heavy), -most, most).astype(held_as)


def setup_inputs(seed: int = 0) -> dict:
    key_of = jax.random.split(jax.random.key(seed), 9)
    return {
        "node_feats": gaussian_with(key_of[0], (NODES, D), 1.0, 24.0, ((0, 256),), (0, 1, 256, 6.0)),
        "grad_out": gaussian_with(key_of[1], (NODES, D), 1.0, 24.0, ((0, 256),), (0, 1, 256, 6.0)),
        "log_sum_exp": jnp.clip(7.5 + 1.5 * jax.random.uniform(key_of[2], (H, NODES), jnp.float32) ** level_of(key_of[2], (H, NODES), ((1, 256),), -0.2, 0.2), 7.5, 9.0),
        "w_query": noise(key_of[3], (D, D), D ** -0.5, 0.25),
        "w_key": noise(key_of[4], (D, D), D ** -0.5, 0.25),
        "w_value": noise(key_of[5], (D, D), D ** -0.5, 0.25),
        "w_output": noise(key_of[6], (D, D), D ** -0.5, 0.25),
        "partners": draw_partners(jax.random.fold_in(key_of[8], 71), 0),
    }


def block_terms(query_blk, key_rows, value_rows, dout_blk, lse_blk):
    scaling = HD ** -0.5
    query_f = query_blk.astype(jnp.float32).reshape(BLOCK, H, HD)
    key_f = key_rows.astype(jnp.float32).reshape(4 * BLOCK, H, HD)
    value_f = value_rows.astype(jnp.float32).reshape(4 * BLOCK, H, HD)
    dout_f = dout_blk.astype(jnp.float32).reshape(BLOCK, H, HD)
    scores = jnp.einsum('ihe,jhe->hij', query_f, key_f) * scaling
    probs = jnp.exp(jnp.minimum(scores - lse_blk[:, :, None], 0.0))
    probs_low = probs.astype(jnp.bfloat16)
    probs_back = probs_low.astype(jnp.float32)
    out_blk = jnp.einsum('hij,jhe->ihe', probs_back, value_f).reshape(BLOCK, D).astype(jnp.bfloat16)
    row_delta = jnp.sum(dout_f * out_blk.astype(jnp.float32).reshape(BLOCK, H, HD), axis=-1).T
    grad_probs = jnp.einsum('ihe,jhe->hij', dout_f, value_f)
    grad_scores = (probs * (grad_probs - row_delta[:, :, None]) * scaling).astype(jnp.bfloat16)
    grad_float = grad_scores.astype(jnp.float32)
    grad_q = jnp.einsum('hij,jhe->ihe', grad_float, key_f).reshape(BLOCK, D).astype(jnp.bfloat16)
    grad_k = jnp.einsum('hij,ihe->jhe', grad_float, query_f).reshape(4, BLOCK, D)
    grad_v = jnp.einsum('hij,ihe->jhe', probs_back, dout_f).reshape(4, BLOCK, D)
    return grad_q, out_blk, grad_k, grad_v


def reference(node_feats, grad_out, log_sum_exp, w_query, w_key, w_value, w_output, partners):
    query = jnp.dot(node_feats, w_query, preferred_element_type=jnp.float32).astype(jnp.bfloat16)
    key_all = jnp.dot(node_feats, w_key, preferred_element_type=jnp.float32).astype(jnp.bfloat16)
    value_all = jnp.dot(node_feats, w_value, preferred_element_type=jnp.float32).astype(jnp.bfloat16)
    d_out = jnp.dot(grad_out, w_output.T, preferred_element_type=jnp.float32).astype(jnp.bfloat16)
    query_blocks = query.reshape(NB, BLOCK, D)
    key_blocks = key_all.reshape(NB, BLOCK, D)
    value_blocks = value_all.reshape(NB, BLOCK, D)
    dout_blocks = d_out.reshape(NB, BLOCK, D)
    lse_blocks = log_sum_exp.reshape(H, NB, BLOCK).transpose(1, 0, 2)

    def step(carry, index):
        acc_key, acc_value = carry
        members = jnp.concatenate([index[None], partners[index]]).astype(jnp.int32)
        key_rows = key_blocks[members].reshape(4 * BLOCK, D)
        value_rows = value_blocks[members].reshape(4 * BLOCK, D)
        grad_q, out_blk, grad_k, grad_v = block_terms(query_blocks[index], key_rows, value_rows, dout_blocks[index], lse_blocks[index])
        acc_key = acc_key.at[members].add(grad_k)
        acc_value = acc_value.at[members].add(grad_v)
        return (acc_key, acc_value), (grad_q, out_blk)

    start = (jnp.zeros((NB, BLOCK, D), jnp.float32), jnp.zeros((NB, BLOCK, D), jnp.float32))
    (acc_key, acc_value), (grad_q, out_all) = lax.scan(step, start, jnp.arange(NB, dtype=jnp.int32))
    grad_query = grad_q.reshape(NODES, D)
    out_rows = out_all.reshape(NODES, D)
    grad_key = acc_key.reshape(NODES, D).astype(jnp.bfloat16)
    grad_value = acc_value.reshape(NODES, D).astype(jnp.bfloat16)
    weight_grads = jnp.concatenate([
        jnp.dot(node_feats.T, grad_query, preferred_element_type=jnp.float32),
        jnp.dot(node_feats.T, grad_key, preferred_element_type=jnp.float32),
        jnp.dot(node_feats.T, grad_value, preferred_element_type=jnp.float32),
        jnp.dot(out_rows.T, grad_out, preferred_element_type=jnp.float32)], axis=1)
    total = jnp.dot(grad_query, w_query.T, preferred_element_type=jnp.float32)
    total = total + jnp.dot(grad_key, w_key.T, preferred_element_type=jnp.float32)
    total = total + jnp.dot(grad_value, w_value.T, preferred_element_type=jnp.float32)
    return total.astype(jnp.bfloat16), weight_grads
```

```python
import jax
import jax.numpy as jnp
from jax import lax
from jax.experimental import pallas as pl
from jax.experimental.pallas import tpu as pltpu
from jax.sharding import PartitionSpec as P


def spread_kernel(x_ref, o_ref, send_sem, recv_sem):
    gx = lax.axis_index("gx")
    gy = lax.axis_index("gy")
    inner = lax.axis_size("gy")
    count = lax.axis_size("gx") * inner
    me = gx * inner + gy
    barrier = pltpu.get_barrier_semaphore()

    def greet(step, carry):
        peer = lax.rem(me + step, count)
        pl.semaphore_signal(
            barrier,
            inc=1,
            device_id=(lax.div(peer, inner), lax.rem(peer, inner)),
            device_id_type=pl.DeviceIdType.MESH,
        )
        return carry

    lax.fori_loop(1, count, greet, 0)
    pl.semaphore_wait(barrier, count - 1)

    def send(step, carry):
        peer = lax.rem(me + step, count)
        pltpu.make_async_remote_copy(
            src_ref=x_ref.at[peer],
            dst_ref=o_ref.at[me],
            send_sem=send_sem,
            recv_sem=recv_sem,
            device_id=(lax.div(peer, inner), lax.rem(peer, inner)),
            device_id_type=pl.DeviceIdType.MESH,
        ).start()
        return carry

    lax.fori_loop(1, count, send, 0)
    pltpu.make_async_copy(x_ref.at[me], o_ref.at[me], recv_sem).start()
    pltpu.make_async_copy(o_ref, o_ref, recv_sem).wait()
    sent = x_ref.at[pl.ds(0, count - 1)]
    pltpu.make_async_copy(sent, sent, send_sem).wait()


def spread_call(x, cid):
    return pl.pallas_call(
        spread_kernel,
        out_shape=jax.ShapeDtypeStruct(x.shape, x.dtype),
        in_specs=[pl.BlockSpec(memory_space=pltpu.VMEM)],
        out_specs=pl.BlockSpec(memory_space=pltpu.VMEM),
        scratch_shapes=[pltpu.SemaphoreType.DMA, pltpu.SemaphoreType.DMA],
        compiler_params=pltpu.CompilerParams(collective_id=cid, has_side_effects=True),
    )(x)


def direct(payload, cid):
    lead, n_outer, n_inner, piece, cols = payload.shape
    rows = payload.astype(jnp.bfloat16).reshape(lead, n_outer * n_inner, 8, cols // 8)
    moved = spread_call(rows.transpose(1, 0, 2, 3), cid)
    return moved.transpose(1, 0, 2, 3).reshape(payload.shape)


def to_pieces(payload):
    n_outer = lax.axis_size("gx")
    n_inner = lax.axis_size("gy")
    rows = payload.shape[1]
    piece_len = rows // (n_outer * n_inner)
    return payload.reshape(payload.shape[0], n_outer, n_inner, piece_len, payload.shape[2])


def fetch_rows(payload, partners):
    lead, rows, cols = payload.shape
    blocks = partners.shape[0]
    piece_len = rows // blocks
    spread = direct(to_pieces(payload), 0).reshape(lead, blocks, piece_len, cols)
    chosen = spread[:, partners.T]
    chosen = chosen.reshape(lead * 3, lax.axis_size("gx"), lax.axis_size("gy"), piece_len, cols)
    back = direct(chosen, 1)
    return back.reshape(lead, 3, rows, cols)


def return_terms(terms, partners):
    lead, rows, cols = terms.shape
    blocks = partners.shape[0]
    piece_len = rows // blocks
    spread = direct(to_pieces(terms), 2).reshape(lead, blocks, piece_len, cols)
    chosen = jnp.stack([spread[match_idx][partners[:, match_idx]] for match_idx in range(3)])
    chosen = chosen.reshape(lead, lax.axis_size("gx"), lax.axis_size("gy"), piece_len, cols)
    back = direct(chosen, 3).astype(jnp.float32).reshape(lead, rows, cols)
    return jnp.sum(back, axis=0)


def attend(query, key_rows, value_rows, d_out, log_sum_exp, head_size, scaling):
    head_count = log_sum_exp.shape[0]
    grad_q_list, out_list, grad_k_list, grad_v_list, delta_list = ([], [], [], [], [])
    for head_idx in range(head_count):
        lo_col = head_idx * head_size
        hi_col = lo_col + head_size
        query_cols = query[:, lo_col:hi_col]
        key_cols = key_rows[:, lo_col:hi_col]
        value_cols = value_rows[:, lo_col:hi_col]
        dout_cols = d_out[:, lo_col:hi_col]
        scores = jnp.dot(query_cols, key_cols.T, preferred_element_type=jnp.float32) * scaling
        probs = jnp.exp(jnp.minimum(scores - log_sum_exp[head_idx][:, None], 0.0))
        probs_low = probs.astype(jnp.bfloat16)
        out_cols = jnp.dot(probs_low, value_cols, preferred_element_type=jnp.float32).astype(
            jnp.bfloat16
        )
        row_delta = jnp.sum(dout_cols.astype(jnp.float32) * out_cols.astype(jnp.float32), axis=-1)
        grad_probs = jnp.dot(dout_cols, value_cols.T, preferred_element_type=jnp.float32)
        grad_scores = (probs * (grad_probs - row_delta[:, None]) * scaling).astype(jnp.bfloat16)
        grad_q_list.append(
            jnp.dot(grad_scores, key_cols, preferred_element_type=jnp.float32).astype(jnp.bfloat16)
        )
        out_list.append(out_cols)
        grad_k_list.append(jnp.dot(grad_scores.T, query_cols, preferred_element_type=jnp.float32))
        grad_v_list.append(jnp.dot(probs_low.T, dout_cols, preferred_element_type=jnp.float32))
        delta_list.append(row_delta)
    return (
        jnp.concatenate(grad_q_list, axis=1),
        jnp.concatenate(out_list, axis=1),
        jnp.concatenate(grad_k_list, axis=1),
        jnp.concatenate(grad_v_list, axis=1),
        jnp.stack(delta_list),
    )


def on_device(node_feats, grad_out, log_sum_exp, w_query, w_key, w_value, w_output, partners):
    block_len, width = node_feats.shape
    head_count = log_sum_exp.shape[0]
    head_size = width // head_count
    scaling = head_size ** (-0.5)
    query = jnp.dot(node_feats, w_query, preferred_element_type=jnp.float32).astype(jnp.bfloat16)
    key_own = jnp.dot(node_feats, w_key, preferred_element_type=jnp.float32).astype(jnp.bfloat16)
    value_own = jnp.dot(node_feats, w_value, preferred_element_type=jnp.float32).astype(
        jnp.bfloat16
    )
    d_out = jnp.dot(grad_out, w_output.T, preferred_element_type=jnp.float32).astype(jnp.bfloat16)
    payload = jnp.concatenate([key_own, value_own], axis=1)[None]
    fetched = fetch_rows(payload, partners)[0]
    key_far = fetched[:, :, :width].reshape(3 * block_len, width)
    value_far = fetched[:, :, width : 2 * width].reshape(3 * block_len, width)
    key_rows = jnp.concatenate([key_own, key_far], axis=0)
    value_rows = jnp.concatenate([value_own, value_far], axis=0)
    grad_query, out_rows, grad_key_all, grad_value_all, row_delta = attend(
        query, key_rows, value_rows, d_out, log_sum_exp, head_size, scaling
    )
    terms = jnp.concatenate(
        [
            grad_key_all[block_len:].reshape(3, block_len, width),
            grad_value_all[block_len:].reshape(3, block_len, width),
        ],
        axis=2,
    )
    returned = return_terms(terms, partners)
    key_total = grad_key_all[:block_len] + returned[:, :width]
    value_total = grad_value_all[:block_len] + returned[:, width:]
    grad_key = key_total.astype(jnp.bfloat16)
    grad_value = value_total.astype(jnp.bfloat16)
    local_weights = jnp.concatenate(
        [
            jnp.dot(node_feats.T, grad_query, preferred_element_type=jnp.float32),
            jnp.dot(node_feats.T, grad_key, preferred_element_type=jnp.float32),
            jnp.dot(node_feats.T, grad_value, preferred_element_type=jnp.float32),
            jnp.dot(out_rows.T, grad_out, preferred_element_type=jnp.float32),
        ],
        axis=1,
    )
    partial_cols = lax.psum_scatter(
        local_weights.astype(jnp.bfloat16), "gy", scatter_dimension=1, tiled=True
    )
    weight_grads = lax.psum_scatter(partial_cols, "gx", scatter_dimension=0, tiled=True).astype(
        jnp.float32
    )
    total = jnp.dot(grad_query, w_query.T, preferred_element_type=jnp.float32)
    total = total + jnp.dot(grad_key, w_key.T, preferred_element_type=jnp.float32)
    total = total + jnp.dot(grad_value, w_value.T, preferred_element_type=jnp.float32)
    return (total.astype(jnp.bfloat16), weight_grads)


def solution(mesh):
    return jax.shard_map(
        on_device,
        mesh=mesh,
        in_specs=(
            P(("gx", "gy"), None),
            P(("gx", "gy"), None),
            P(None, ("gx", "gy")),
            P(),
            P(),
            P(),
            P(),
            P(),
        ),
        out_specs=(P(("gx", "gy"), None), P("gx", "gy")),
        check_vma=False,
    )
```

```python
import functools

import jax
import jax.numpy as jnp
from jax import lax
from jax.experimental import pallas as pl
from jax.experimental.pallas import tpu as pltpu
from jax.sharding import PartitionSpec as P

MESH = pl.DeviceIdType.MESH
F32 = jnp.float32
BF16 = jnp.bfloat16
DEVICES = 256
PIECES = 128
LIMIT = 60 * 1024 * 1024


def nt(a, b):
    return lax.dot_general(a, b, (((1,), (1,)), ((), ())), preferred_element_type=F32)


def nn(a, b):
    return lax.dot_general(a, b, (((1,), (0,)), ((), ())), preferred_element_type=F32)


def position():
    gx = lax.axis_index("gx")
    gy = lax.axis_index("gy")
    x = lax.rem(gx, 4)
    y = lax.rem(lax.div(gy, 2), 4)
    z = lax.div(gx, 4) + 2 * lax.div(gy, 8)
    core = lax.rem(gy, 2)
    return x, y, z, core


def place(x, y, z, core):
    return lax.rem(z, 2) * 4 + x, (lax.div(z, 2) * 4 + y) * 2 + core


def greet_all(barrier, gx, gy):
    me = gx * 32 + gy

    def greet(step, carry):
        peer = lax.rem(me + step, DEVICES)
        pl.semaphore_signal(
            barrier,
            inc=1,
            device_id=(lax.div(peer, 32), lax.rem(peer, 32)),
            device_id_type=MESH,
        )
        return carry

    lax.fori_loop(1, DEVICES, greet, 0)


def spread(src_of, dst, gx, gy, send_sem, recv_sem):
    me = gx * 32 + gy

    def send(step, carry):
        peer = lax.rem(me + step, DEVICES)
        tx = lax.div(peer, 32)
        ty = lax.rem(peer, 32)
        pltpu.make_async_remote_copy(
            src_ref=src_of(tx, ty),
            dst_ref=dst.at[me],
            send_sem=send_sem,
            recv_sem=recv_sem,
            device_id=(tx, ty),
            device_id_type=MESH,
        ).start()
        return carry

    lax.fori_loop(1, DEVICES, send, 0)
    pltpu.make_async_copy(src_of(gx, gy), dst.at[me], recv_sem).start()


def drain(ref, sem):
    pltpu.make_async_copy(ref, ref, sem).wait()


def piece_of(tx, ty):
    return tx * 16 + lax.rem(ty, 16)


def small_of(tx, ty):
    return (lax.div(tx, 4) * 2 + lax.rem(tx, 2)) * 4 + lax.rem(ty, 4)


def wide_target(index):
    x, y, z, core = position()
    dz = lax.div(index, 32)
    tz = lax.rem(z + dz + 7 - core, 8)
    tx = lax.rem(x + lax.rem(index, 4), 4)
    ty = lax.rem(y + lax.rem(lax.div(index, 4), 4), 4)
    tc = lax.rem(core + lax.rem(lax.div(index, 16), 2), 2)
    return place(tx, ty, tz, tc)


def small_target(index):
    x, y, z, core = position()
    tx = lax.div(x, 2) * 2 + lax.rem(x + lax.rem(index, 2), 2)
    ty = lax.div(y, 2) * 2 + lax.rem(y + lax.rem(lax.div(index, 2), 2), 2)
    tz = lax.div(z, 2) * 2 + lax.rem(z + lax.rem(lax.div(index, 4), 2), 2)
    tc = lax.rem(core + lax.div(index, 8), 2)
    return place(tx, ty, tz, tc)


def choose(target, count, partners_ref, held, chosen):
    def pick(index, carry):
        tx, ty = target(index)
        base = (tx * 32 + ty) * 3
        for j in range(3):
            chosen[index, j] = held[partners_ref[base + j]]
        return carry

    lax.fori_loop(0, count, pick, 0)


def deliver(target, count, self_index, slot, chosen, dst, send_sem, recv_sem):
    def send(index, carry):
        tx, ty = target(index)
        pltpu.make_async_remote_copy(
            src_ref=chosen.at[index],
            dst_ref=dst.at[slot],
            send_sem=send_sem,
            recv_sem=recv_sem,
            device_id=(tx, ty),
            device_id_type=MESH,
        ).start()
        return carry

    lax.fori_loop(0, self_index, send, 0)
    lax.fori_loop(self_index + 1, count, send, 0)
    pltpu.make_async_copy(chosen.at[self_index], dst.at[slot], recv_sem).start()


def fetch_kernel(partners_ref, feats, gouts, lses, far_x, far_g, far_l,
                 held_x, held_g, held_l, pick_x, pick_g, pick_l, send, recv):
    gx = lax.axis_index("gx")
    gy = lax.axis_index("gy")
    core = lax.rem(gy, 2)
    barrier = pltpu.get_barrier_semaphore()
    greet_all(barrier, gx, gy)
    pl.semaphore_wait(barrier, DEVICES - 1)
    spread(lambda tx, ty: feats.at[piece_of(tx, ty)], held_x, gx, gy, send.at[0], recv.at[0])
    spread(lambda tx, ty: gouts.at[piece_of(tx, ty)], held_g, gx, gy, send.at[1], recv.at[1])
    spread(lambda tx, ty: lses.at[small_of(tx, ty)], held_l, gx, gy, send.at[2], recv.at[2])
    home = (1 + core) * 32
    drain(held_x, recv.at[0])
    choose(wide_target, PIECES, partners_ref, held_x, pick_x)
    deliver(wide_target, PIECES, home, piece_of(gx, gy), pick_x, far_x, send.at[3], recv.at[3])
    drain(held_g, recv.at[1])
    choose(wide_target, PIECES, partners_ref, held_g, pick_g)
    deliver(wide_target, PIECES, home, piece_of(gx, gy), pick_g, far_g, send.at[4], recv.at[4])
    drain(held_l, recv.at[2])
    choose(small_target, 16, partners_ref, held_l, pick_l)
    deliver(small_target, 16, 0, small_of(gx, gy), pick_l, far_l, send.at[5], recv.at[5])
    drain(far_x, recv.at[3])
    drain(far_g, recv.at[4])
    drain(far_l, recv.at[5])
    for k, ref in enumerate((held_x, held_g, held_l)):
        drain(ref.at[pl.ds(0, DEVICES - 1)], send.at[k])
    for k, ref in enumerate((far_x, far_g)):
        drain(ref.at[pl.ds(0, PIECES - 1)], send.at[3 + k])
    drain(far_l.at[pl.ds(0, 15)], send.at[5])


def project(w, src, dst, rows, scale=None, transposed=False):
    full = nt(src, w[...]) if transposed else nn(src, w[...])
    low = full.astype(BF16)
    if scale is not None:
        low = low * jnp.asarray(scale, BF16)
    for p in range(4):
        dst[p, rows, :] = low[:, 128 * p : 128 * (p + 1)]


def unpack(far, j):
    return jnp.concatenate([far[32 * c : 32 * (c + 1), j].reshape(256, 128) for c in range(4)], axis=1)


def half_mask(half):
    lane = lax.broadcasted_iota(jnp.int32, (1, 128), 1)
    return (lane < 64) if half == 0 else (lane >= 64)


def forward_head(p, half, lse_col, q_all, k_all, v_all, d_all, prob):
    mask = half_mask(half)
    zero = jnp.zeros((), BF16)
    q_own = jnp.where(mask, q_all[p, 0:256, :], zero)
    d_own = jnp.where(mask, d_all[p, 0:256, :], zero)
    score = nt(q_own, k_all[p])
    prob[...] = jnp.exp(jnp.minimum(score - lse_col, 0.0))
    out = nn(prob[...].astype(BF16), v_all[p]).astype(BF16)
    delta = jnp.sum(d_own.astype(F32) * out.astype(F32), axis=1, keepdims=True)
    grad_prob = nt(d_own, v_all[p])
    grad_score = (prob[...] * (grad_prob - delta)).astype(BF16)
    grad_q = (nn(grad_score, k_all[p]) * 0.125).astype(BF16)
    return out, grad_q, delta


def reverse_head(p, half, lse_row, delta_row, q_all, k_all, v_all, d_all):
    mask = half_mask(half)
    zero = jnp.zeros((), BF16)
    k_own = jnp.where(mask, k_all[p, 0:256, :], zero)
    v_own = jnp.where(mask, v_all[p, 0:256, :], zero)
    score = nt(k_own, q_all[p])
    prob = jnp.exp(jnp.minimum(score - lse_row, 0.0))
    grad_prob = nt(v_own, d_all[p])
    grad_score = (prob * (grad_prob - delta_row)).astype(BF16)
    grad_v = nn(prob.astype(BF16), d_all[p]).astype(BF16)
    grad_k = nn(grad_score, q_all[p]).astype(BF16)
    return grad_k, grad_v


def forward_kernel(x, g, lse, far_x, far_g, wq, wk, wv, wo,
                   q_all, k_all, v_all, d_all, grad_q, out, deltas,
                   prob, lse_cols, delta_cols):
    for j in range(4):
        rows = pl.ds(256 * j, 256)
        src = x[...] if j == 0 else unpack(far_x, j - 1)
        top = g[...] if j == 0 else unpack(far_g, j - 1)
        project(wq, src, q_all, rows, scale=0.125)
        project(wk, src, k_all, rows)
        project(wv, src, v_all, rows)
        project(wo, top, d_all, rows, transposed=True)
    turned = jnp.transpose(lse[...], (1, 0))
    for h in range(8):
        lse_cols[h] = turned[:, h : h + 1]

    def pair(p, carry):
        o0, q0, e0 = forward_head(p, 0, lse_cols[2 * p], q_all, k_all, v_all, d_all, prob)
        o1, q1, e1 = forward_head(p, 1, lse_cols[2 * p + 1], q_all, k_all, v_all, d_all, prob)
        mask = half_mask(0)
        out[p] = jnp.where(mask, o0, o1)
        grad_q[p] = jnp.where(mask, q0, q1)
        delta_cols[2 * p] = e0
        delta_cols[2 * p + 1] = e1
        return carry

    lax.fori_loop(0, 4, pair, 0)
    lane = lax.broadcasted_iota(jnp.int32, (256, 128), 1)
    flat = jnp.zeros((256, 128), F32)
    for h in range(8):
        flat = jnp.where(lane == h, delta_cols[h], flat)
    turned = jnp.transpose(flat, (1, 0))
    for h in range(8):
        for half in range(2):
            deltas[2 * h + half] = turned[h : h + 1, 128 * half : 128 * (half + 1)]


def delta_kernel(partners_ref, deltas, far_d, held, pick, send, recv):
    gx = lax.axis_index("gx")
    gy = lax.axis_index("gy")
    barrier = pltpu.get_barrier_semaphore()
    greet_all(barrier, gx, gy)
    pl.semaphore_wait(barrier, DEVICES - 1)
    spread(lambda tx, ty: deltas.at[small_of(tx, ty)], held, gx, gy, send.at[0], recv.at[0])
    drain(held, recv.at[0])
    choose(small_target, 16, partners_ref, held, pick)
    deliver(small_target, 16, 0, small_of(gx, gy), pick, far_d, send.at[1], recv.at[1])
    drain(far_d, recv.at[1])
    drain(held.at[pl.ds(0, DEVICES - 1)], send.at[0])
    drain(far_d.at[pl.ds(0, 15)], send.at[1])


def fill_rows(dst, own, far):
    for h in range(8):
        for half in range(2):
            dst[h, :, 128 * half : 128 * (half + 1)] = own[2 * h + half]
            for j in range(3):
                lo = 256 * (j + 1) + 128 * half
                dst[h, :, lo : lo + 128] = far[2 * h + half, j]


def reverse_kernel(x, g, lses, deltas, far_l, far_d, q_all, k_all, v_all, d_all, grad_q, out,
                   wq, wk, wv, grad_nodes, terms, lse_rows, delta_rows, grad_k, grad_v):
    fill_rows(lse_rows, lses, far_l)
    fill_rows(delta_rows, deltas, far_d)

    def pair(p, carry):
        k0, v0 = reverse_head(p, 0, lse_rows[2 * p], delta_rows[2 * p], q_all, k_all, v_all, d_all)
        k1, v1 = reverse_head(p, 1, lse_rows[2 * p + 1], delta_rows[2 * p + 1], q_all, k_all, v_all, d_all)
        mask = half_mask(0)
        grad_k[p] = jnp.where(mask, k0, k1)
        grad_v[p] = jnp.where(mask, v0, v1)
        return carry

    lax.fori_loop(0, 4, pair, 0)
    total = jnp.zeros((256, 512), F32)
    for grad, w in ((grad_q, wq), (grad_k, wk), (grad_v, wv)):
        joined = jnp.concatenate([grad[p] for p in range(4)], axis=1)
        total = total + nt(joined, w[...])
    grad_nodes[...] = total.astype(BF16)
    turned = jnp.transpose(x[...], (1, 0))
    top = g[...]
    joined = jnp.concatenate([out[p] for p in range(4)], axis=1)
    out_turned = jnp.transpose(joined, (1, 0))
    for m in range(4):
        for p in range(4):
            if m < 3:
                term = nn(turned, (grad_q, grad_k, grad_v)[m][p])
            else:
                term = nn(out_turned, top[:, 128 * p : 128 * (p + 1)])
            split = term.astype(BF16).reshape(2, 4, 2, 32, 128)
            for c in range(2):
                for zl in range(2):
                    terms[c, p, :, m, zl] = split[zl, :, c]


def reduce_kernel(terms, result, got_core, sum_core, got_plane, sum_plane, got_line, mine, got_last, send, recv):
    x, y, z, core = position()
    barrier = pltpu.get_barrier_semaphore()

    def hello(tx, ty, tz, tc):
        pl.semaphore_signal(barrier, inc=1, device_id=place(tx, ty, tz, tc), device_id_type=MESH)

    hello(x, y, z, 1 - core)
    lax.fori_loop(1, 16, lambda i, c: (hello(lax.rem(x + lax.rem(i, 4), 4), lax.rem(y + lax.div(i, 4), 4), z, core), c)[1], 0)
    lax.fori_loop(1, 8, lambda i, c: (hello(x, y, lax.rem(z + i, 8), core), c)[1], 0)
    pl.semaphore_wait(barrier, 23)
    step = pltpu.make_async_remote_copy(
        src_ref=terms.at[1 - core], dst_ref=got_core, send_sem=send.at[0], recv_sem=recv.at[0],
        device_id=place(x, y, z, 1 - core), device_id_type=MESH)
    step.start()
    step.wait()
    for p in range(4):
        sum_core[p] = (terms[core, p].astype(F32) + got_core[p].astype(F32)).astype(BF16)

    def to_plane(i, carry):
        tx = lax.rem(x + lax.rem(i, 4), 4)
        ty = lax.rem(y + lax.div(i, 4), 4)
        pltpu.make_async_remote_copy(
            src_ref=sum_core.at[ty, tx], dst_ref=got_plane.at[i], send_sem=send.at[1], recv_sem=recv.at[1],
            device_id=place(tx, ty, z, core), device_id_type=MESH).start()
        return carry

    lax.fori_loop(1, 16, to_plane, 0)
    others = got_plane.at[pl.ds(1, 15)]
    drain(others, recv.at[1])
    total = sum_core[y, x].astype(F32)
    for i in range(1, 16):
        total = total + got_plane[i].astype(F32)
    sum_plane[...] = total.reshape(8, 32, 128).astype(BF16)

    def to_line(i, carry):
        tz = lax.rem(z + i, 8)
        slot = lax.div(tz, 2) * 2 + lax.rem(tz, 2)
        pltpu.make_async_remote_copy(
            src_ref=sum_plane.at[slot], dst_ref=got_line.at[i], send_sem=send.at[2], recv_sem=recv.at[2],
            device_id=place(x, y, tz, core), device_id_type=MESH).start()
        return carry

    lax.fori_loop(1, 8, to_line, 0)
    drain(got_line.at[pl.ds(1, 7)], recv.at[2])
    total = sum_plane[z].astype(F32)
    for i in range(1, 8):
        total = total + got_line[i].astype(F32)
    mine[...] = total
    last = pltpu.make_async_remote_copy(
        src_ref=mine, dst_ref=got_last, send_sem=send.at[3], recv_sem=recv.at[3],
        device_id=place(x, y, z, 1 - core), device_id_type=MESH)
    last.start()
    last.wait()
    first = jnp.where(core == 0, mine[...], got_last[...])
    second = jnp.where(core == 0, got_last[...], mine[...])
    both = jnp.concatenate([first, second], axis=0)
    result[...] = jnp.where(core == 0, both[:, :64], both[:, 64:])
    drain(others, send.at[1])
    drain(got_line.at[pl.ds(1, 7)], send.at[2])


def vmem(count):
    return [pl.BlockSpec(memory_space=pltpu.VMEM)] * count


def sds(shape, kind):
    return jax.ShapeDtypeStruct(shape, kind)


def params(cid=None):
    if cid is None:
        return pltpu.CompilerParams(vmem_limit_bytes=LIMIT)
    return pltpu.CompilerParams(vmem_limit_bytes=LIMIT, collective_id=cid, has_side_effects=True)


def pieces(rows):
    return rows.reshape(32, 8, 4, 128).transpose(2, 0, 1, 3).reshape(128, 8, 128)


def on_device(x, g, lse, wq, wk, wv, wo, partners):
    flat = partners.reshape(-1)
    lses = lse.reshape(16, 1, 128)
    smem = pl.BlockSpec(memory_space=pltpu.SMEM)
    dma = pltpu.SemaphoreType.DMA
    wide = (PIECES, 3, 8, 128)
    small = (16, 3, 1, 128)
    far_x, far_g, far_l = pl.pallas_call(
        fetch_kernel,
        out_shape=(sds(wide, BF16), sds(wide, BF16), sds(small, F32)),
        in_specs=[smem] + vmem(3),
        out_specs=tuple(vmem(3)),
        scratch_shapes=[
            pltpu.VMEM((DEVICES, 8, 128), BF16), pltpu.VMEM((DEVICES, 8, 128), BF16), pltpu.VMEM((DEVICES, 1, 128), F32),
            pltpu.VMEM(wide, BF16), pltpu.VMEM(wide, BF16), pltpu.VMEM(small, F32),
            dma((6,)), dma((6,)),
        ],
        compiler_params=params(0),
        name="fetch",
    )(flat, pieces(x), pieces(g), lses)
    split = sds((4, 1024, 128), BF16)
    q_all, k_all, v_all, d_all, grad_q, out, deltas = pl.pallas_call(
        forward_kernel,
        out_shape=(split,) * 4 + (sds((4, 256, 128), BF16),) * 2 + (sds((16, 1, 128), F32),),
        in_specs=vmem(9),
        out_specs=tuple(vmem(7)),
        scratch_shapes=[pltpu.VMEM((256, 1024), F32), pltpu.VMEM((8, 256, 1), F32), pltpu.VMEM((8, 256, 1), F32)],
        compiler_params=params(),
        name="forward",
    )(x, g, lse, far_x, far_g, wq, wk, wv, wo)
    far_d = pl.pallas_call(
        delta_kernel,
        out_shape=sds(small, F32),
        in_specs=[smem] + vmem(1),
        out_specs=vmem(1)[0],
        scratch_shapes=[pltpu.VMEM((DEVICES, 1, 128), F32), pltpu.VMEM(small, F32), dma((2,)), dma((2,))],
        compiler_params=params(1),
        name="delta",
    )(flat, deltas)
    grad_nodes, terms = pl.pallas_call(
        reverse_kernel,
        out_shape=(sds((256, 512), BF16), sds((2, 4, 4, 4, 2, 32, 128), BF16)),
        in_specs=vmem(15),
        out_specs=tuple(vmem(2)),
        scratch_shapes=[pltpu.VMEM((8, 1, 1024), F32), pltpu.VMEM((8, 1, 1024), F32),
                        pltpu.VMEM((4, 256, 128), BF16), pltpu.VMEM((4, 256, 128), BF16)],
        compiler_params=params(),
        name="reverse",
    )(x, g, lses, deltas, far_l, far_d, q_all, k_all, v_all, d_all, grad_q, out, wq, wk, wv)
    result = pl.pallas_call(
        reduce_kernel,
        out_shape=sds((64, 64), F32),
        in_specs=vmem(1),
        out_specs=vmem(1)[0],
        scratch_shapes=[
            pltpu.VMEM((4, 4, 4, 2, 32, 128), BF16), pltpu.VMEM((4, 4, 4, 2, 32, 128), BF16),
            pltpu.VMEM((16, 4, 2, 32, 128), BF16), pltpu.VMEM((8, 32, 128), BF16),
            pltpu.VMEM((8, 32, 128), BF16), pltpu.VMEM((32, 128), F32), pltpu.VMEM((32, 128), F32),
            dma((4,)), dma((4,)),
        ],
        compiler_params=params(2),
        name="reduce",
    )(terms)
    return grad_nodes, result


def solution(mesh):
    return jax.shard_map(
        on_device,
        mesh=mesh,
        in_specs=(
            P(("gx", "gy"), None),
            P(("gx", "gy"), None),
            P(None, ("gx", "gy")),
            P(),
            P(),
            P(),
            P(),
            P(),
        ),
        out_specs=(P(("gx", "gy"), None), P("gx", "gy")),
        check_vma=False,
    )
```

```python
import functools

import jax
import jax.numpy as jnp
from jax import lax
from jax.experimental import pallas as pl
from jax.experimental.pallas import tpu as pltpu
from jax.sharding import PartitionSpec as P

MESH = pl.DeviceIdType.MESH
F32 = jnp.float32
BF16 = jnp.bfloat16
DEVICES = 256
PIECES = 128
LIMIT = 60 * 1024 * 1024


def nt(a, b):
    return lax.dot_general(a, b, (((1,), (1,)), ((), ())), preferred_element_type=F32)


def nn(a, b):
    return lax.dot_general(a, b, (((1,), (0,)), ((), ())), preferred_element_type=F32)


def position():
    gx = lax.axis_index("gx")
    gy = lax.axis_index("gy")
    x = lax.rem(gx, 4)
    y = lax.rem(lax.div(gy, 2), 4)
    z = lax.div(gx, 4) + 2 * lax.div(gy, 8)
    core = lax.rem(gy, 2)
    return x, y, z, core


def place(x, y, z, core):
    return lax.rem(z, 2) * 4 + x, (lax.div(z, 2) * 4 + y) * 2 + core


def rendezvous(barrier, second, third):
    x, y, z, core = position()

    def wide(i):
        return place(lax.rem(x + lax.rem(i, 4), 4), y, z, lax.rem(core + lax.div(i, 4), 2))

    def signal(sem, peer):
        pl.semaphore_signal(sem, inc=1, device_id=peer, device_id_type=MESH)

    def first():
        for i in (4, 2, 6, 3, 5, 1, 7):
            signal(barrier, place(x, y, lax.rem(z + i, 8), core))
        for i in (2, 1, 3):
            signal(barrier, place(x, lax.rem(y + i, 4), z, core))
        for i in range(1, 8):
            signal(barrier, wide(i))

    def rest():
        pl.semaphore_wait(barrier, 17)
        for i in range(1, 8):
            signal(second, wide(i))
        pl.semaphore_wait(second, 7)
        for i in range(1, 4):
            signal(third, place(x, lax.rem(y + i, 4), z, core))
        pl.semaphore_wait(third, 3)

    return first, rest


def spread(src_of, dst, gx, gy, send_sem, recv_sem):
    me = gx * 32 + gy

    def send(step, carry):
        peer = lax.rem(me + step, DEVICES)
        tx = lax.div(peer, 32)
        ty = lax.rem(peer, 32)
        pltpu.make_async_remote_copy(
            src_ref=src_of(tx, ty),
            dst_ref=dst.at[me],
            send_sem=send_sem,
            recv_sem=recv_sem,
            device_id=(tx, ty),
            device_id_type=MESH,
        ).start()
        return carry

    lax.fori_loop(1, DEVICES, send, 0)
    pltpu.make_async_copy(src_of(gx, gy), dst.at[me], recv_sem).start()


def drain(ref, sem):
    pltpu.make_async_copy(ref, ref, sem).wait()


def piece_of(tx, ty):
    return tx * 16 + lax.rem(ty, 16)


def small_of(tx, ty):
    return (lax.div(tx, 4) * 2 + lax.rem(tx, 2)) * 4 + lax.rem(ty, 4)


def wide_target(index):
    x, y, z, core = position()
    dz = lax.div(index, 32)
    tz = lax.rem(z + dz + 7 - core, 8)
    tx = lax.rem(x + lax.rem(index, 4), 4)
    ty = lax.rem(y + lax.rem(lax.div(index, 4), 4), 4)
    tc = lax.rem(core + lax.rem(lax.div(index, 16), 2), 2)
    return place(tx, ty, tz, tc)


def small_target(index):
    x, y, z, core = position()
    tx = lax.div(x, 2) * 2 + lax.rem(x + lax.rem(index, 2), 2)
    ty = lax.div(y, 2) * 2 + lax.rem(y + lax.rem(lax.div(index, 2), 2), 2)
    tz = lax.div(z, 2) * 2 + lax.rem(z + lax.rem(lax.div(index, 4), 2), 2)
    tc = lax.rem(core + lax.div(index, 8), 2)
    return place(tx, ty, tz, tc)


def choose(target, count, partners_ref, held, chosen):
    def pick(index, carry):
        tx, ty = target(index)
        block = tx * 32 + ty
        for j in range(3):
            chosen[index, j] = held[partners_ref[block, j]]
        return carry

    lax.fori_loop(0, count, pick, 0)


def deliver(target, count, self_index, slot, chosen, dst, send_sem, recv_sem):
    def send(index, carry):
        tx, ty = target(index)
        pltpu.make_async_remote_copy(
            src_ref=chosen.at[index],
            dst_ref=dst.at[slot],
            send_sem=send_sem,
            recv_sem=recv_sem,
            device_id=(tx, ty),
            device_id_type=MESH,
        ).start()
        return carry

    lax.fori_loop(0, self_index, send, 0)
    lax.fori_loop(self_index + 1, count, send, 0)
    pltpu.make_async_copy(chosen.at[self_index], dst.at[slot], recv_sem).start()


def project(w, src, dst, rows, scale=None, transposed=False):
    full = nt(src, w[...]) if transposed else nn(src, w[...])
    low = full.astype(BF16)
    if scale is not None:
        low = low * jnp.asarray(scale, BF16)
    for p in range(4):
        dst[p, rows, :] = low[:, 128 * p : 128 * (p + 1)]


def unpack(far, j):
    return jnp.concatenate([far[32 * c : 32 * (c + 1), j].reshape(256, 128) for c in range(4)], axis=1)


def half_mask(half):
    lane = lax.broadcasted_iota(jnp.int32, (1, 128), 1)
    return (lane < 64) if half == 0 else (lane >= 64)


def fill_rows(dst, own, far):
    for h in range(8):
        for half in range(2):
            dst[h, :, 128 * half : 128 * (half + 1)] = own[2 * h + half]
            for j in range(3):
                lo = 256 * (j + 1) + 128 * half
                dst[h, :, lo : lo + 128] = far[2 * h + half, j]


def heads(body):
    def pair(p, carry):
        for half in range(2):
            body(p, half, 2 * p + half)
        return carry

    lax.fori_loop(0, 4, pair, 0)


def own_part(ref, p, half):
    return jnp.where(half_mask(half), ref[p, 0:256, :], jnp.zeros((), BF16))


def merge(dst, p, half, value):
    if half == 0:
        dst[p] = value
    else:
        dst[p] = jnp.where(half_mask(0), dst[p], value)


def turn_rows(ref):
    return jnp.transpose(jnp.concatenate([ref[p] for p in range(4)], axis=1), (1, 0))


def weight_term(m, left, right_of, terms):
    def column(p, carry):
        full = nn(left, right_of(p))
        low = full[:256]
        high = full[256:]
        first = half_mask(0)
        even = jnp.where(first, low, pltpu.roll(high, 64, 1))
        odd = jnp.where(first, pltpu.roll(low, 64, 1), high)
        terms[m, 0, p] = even.astype(BF16).reshape(4, 64, 128)
        terms[m, 1, p] = odd.astype(BF16).reshape(4, 64, 128)
        return carry

    lax.fori_loop(0, 4, column, 0)


def plane_peer(i):
    x, y, z, core = position()
    tx = lax.rem(x + lax.rem(i, 4), 4)
    ty = lax.rem(y + lax.rem(lax.div(i, 4), 4), 4)
    tc = lax.rem(core + lax.div(i, 16), 2)
    return tx, ty, z, tc


def to_plane(m, terms, got_plane, send_sem, recv_sem):
    def step(i, carry):
        tx, ty, tz, tc = plane_peer(i)
        pltpu.make_async_remote_copy(
            src_ref=terms.at[m, tc, ty, tx],
            dst_ref=got_plane.at[m, i],
            send_sem=send_sem,
            recv_sem=recv_sem,
            device_id=place(tx, ty, tz, tc),
            device_id_type=MESH,
        ).start()
        return carry

    lax.fori_loop(1, 32, step, 0)


def to_line(m, terms, got_plane, sum_plane, got_line, plane_sem, send_sem, recv_sem):
    x, y, z, core = position()
    drain(got_plane.at[m, pl.ds(1, 31)], plane_sem)

    def add(i, total):
        return total + got_plane[m, i].astype(F32)

    total = lax.fori_loop(1, 32, add, terms[m, core, y, x].astype(F32))
    sum_plane[m] = total.astype(BF16)
    for i in range(2):
        tz = 2 * m + i

        @pl.when(z != tz)
        def _():
            pltpu.make_async_remote_copy(
                src_ref=sum_plane.at[m],
                dst_ref=got_line.at[z],
                send_sem=send_sem,
                recv_sem=recv_sem,
                device_id=place(x, y, tz, core),
                device_id_type=MESH,
            ).start()

        @pl.when(z == tz)
        def _():
            pltpu.make_async_copy(sum_plane.at[m], got_line.at[z], recv_sem).start()


def whole_kernel(partners_ref, x, g, lse, wq, wk, wv, wo, grad_nodes, result,
                 cut_x, cut_g, cut_l, held_x, held_g, held_l, held_d, pick_x, pick_g, pick_l, pick_d,
                 far_x, far_g, far_l, far_d,
                 q_all, k_all, v_all, d_all, prob, grad_prob, prob_t, grad_prob_t,
                 part_out, out, grad_q, grad_k, grad_v, part_v, deltas,
                 lse_cols, delta_cols, lse_rows, delta_rows,
                 terms, got_plane, sum_plane, got_line,
                 second, third, send, recv, plane_send, plane_recv):
    gx = lax.axis_index("gx")
    gy = lax.axis_index("gy")
    zpos = lax.div(gx, 4) + 2 * lax.div(gy, 8)
    core = lax.rem(gy, 2)
    first, rest = rendezvous(pltpu.get_barrier_semaphore(), second, third)
    first()
    for c in range(4):
        cut_x[32 * c : 32 * (c + 1)] = x[:, 128 * c : 128 * (c + 1)].reshape(32, 8, 128)
        cut_g[32 * c : 32 * (c + 1)] = g[:, 128 * c : 128 * (c + 1)].reshape(32, 8, 128)
    for h in range(8):
        for half in range(2):
            cut_l[2 * h + half] = lse[h : h + 1, 128 * half : 128 * (half + 1)]
    rest()
    spread(lambda tx, ty: cut_x.at[piece_of(tx, ty)], held_x, gx, gy, send.at[0], recv.at[0])
    spread(lambda tx, ty: cut_g.at[piece_of(tx, ty)], held_g, gx, gy, send.at[1], recv.at[1])
    spread(lambda tx, ty: cut_l.at[small_of(tx, ty)], held_l, gx, gy, send.at[2], recv.at[2])

    own = pl.ds(0, 256)
    project(wq, x[...], q_all, own, scale=0.125)
    project(wk, x[...], k_all, own)
    project(wv, x[...], v_all, own)
    project(wo, g[...], d_all, own, transposed=True)
    turned = jnp.transpose(lse[...], (1, 0))
    for h in range(8):
        lse_cols[h] = turned[:, h : h + 1]

    home = (1 + core) * 32
    slot = piece_of(gx, gy)
    drain(held_x, recv.at[0])
    choose(wide_target, PIECES, partners_ref, held_x, pick_x)
    deliver(wide_target, PIECES, home, slot, pick_x, far_x, send.at[3], recv.at[3])

    def own_forward(p, half, h):
        score = nt(own_part(q_all, p, half), k_all[p, 0:256, :])
        prob[h, :, 0:256] = jnp.exp(jnp.minimum(score - lse_cols[h], 0.0))
        part_out[h] = nn(prob[h, :, 0:256].astype(BF16), v_all[p, 0:256, :])
        grad_prob[h, :, 0:256] = nt(own_part(d_all, p, half), v_all[p, 0:256, :])

    heads(own_forward)

    drain(held_g, recv.at[1])
    choose(wide_target, PIECES, partners_ref, held_g, pick_g)
    deliver(wide_target, PIECES, home, slot, pick_g, far_g, send.at[4], recv.at[4])
    drain(held_l, recv.at[2])
    choose(small_target, 16, partners_ref, held_l, pick_l)
    deliver(small_target, 16, 0, small_of(gx, gy), pick_l, far_l, send.at[5], recv.at[5])

    def own_reverse(p, half, h):
        score = nt(own_part(k_all, p, half), q_all[p, 0:256, :])
        row = jnp.concatenate([cut_l[2 * h], cut_l[2 * h + 1]], axis=1)
        prob_t[h, :, 0:256] = jnp.exp(jnp.minimum(score - row, 0.0))
        part_v[h] = nn(prob_t[h, :, 0:256].astype(BF16), d_all[p, 0:256, :])
        grad_prob_t[h, :, 0:256] = nt(own_part(v_all, p, half), d_all[p, 0:256, :])

    heads(own_reverse)

    drain(far_x, recv.at[3])
    for j in range(3):
        rows = pl.ds(256 * (j + 1), 256)
        src = unpack(far_x, j)
        project(wk, src, k_all, rows)
        project(wv, src, v_all, rows)
        project(wq, src, q_all, rows, scale=0.125)

    def forward(p, half, h):
        score = nt(own_part(q_all, p, half), k_all[p, 256:, :])
        prob[h, :, 256:] = jnp.exp(jnp.minimum(score - lse_cols[h], 0.0))
        low = (part_out[h] + nn(prob[h, :, 256:].astype(BF16), v_all[p, 256:, :])).astype(BF16)
        d_own = own_part(d_all, p, half)
        grad_prob[h, :, 256:] = nt(d_own, v_all[p, 256:, :])
        delta = jnp.sum(d_own.astype(F32) * low.astype(F32), axis=1, keepdims=True)
        delta_cols[h] = delta
        merge(out, p, half, low)

    heads(forward)
    lane = lax.broadcasted_iota(jnp.int32, (256, 128), 1)
    flat = jnp.zeros((256, 128), F32)
    for h in range(8):
        flat = jnp.where(lane == h, delta_cols[h], flat)
    turned = jnp.transpose(flat, (1, 0))
    for h in range(8):
        for half in range(2):
            deltas[2 * h + half] = turned[h : h + 1, 128 * half : 128 * (half + 1)]
    spread(lambda tx, ty: deltas.at[small_of(tx, ty)], held_d, gx, gy, send.at[6], recv.at[6])

    def forward_grad(p, half, h):
        grad_score = (prob[h] * (grad_prob[h] - delta_cols[h])).astype(BF16)
        merge(grad_q, p, half, (nn(grad_score, k_all[p]) * 0.125).astype(BF16))

    heads(forward_grad)

    drain(held_d, recv.at[6])
    choose(small_target, 16, partners_ref, held_d, pick_d)
    deliver(small_target, 16, 0, small_of(gx, gy), pick_d, far_d, send.at[7], recv.at[7])

    x_turned = jnp.transpose(x[...], (1, 0))
    weight_term(0, x_turned, lambda p: grad_q[p], terms)
    to_plane(0, terms, got_plane, plane_send.at[0], plane_recv.at[0])
    out_turned = turn_rows(out)
    weight_term(3, out_turned, lambda p: g[:, pl.ds(pl.multiple_of(128 * p, 128), 128)], terms)
    to_plane(3, terms, got_plane, plane_send.at[3], plane_recv.at[3])

    drain(far_g, recv.at[4])
    drain(far_l, recv.at[5])
    for j in range(3):
        project(wo, unpack(far_g, j), d_all, pl.ds(256 * (j + 1), 256), transposed=True)
    fill_rows(lse_rows, cut_l, far_l)

    def reverse(p, half, h):
        score = nt(own_part(k_all, p, half), q_all[p, 256:, :])
        prob_t[h, :, 256:] = jnp.exp(jnp.minimum(score - lse_rows[h, :, 256:], 0.0))
        low = (part_v[h] + nn(prob_t[h, :, 256:].astype(BF16), d_all[p, 256:, :])).astype(BF16)
        merge(grad_v, p, half, low)
        grad_prob_t[h, :, 256:] = nt(own_part(v_all, p, half), d_all[p, 256:, :])

    heads(reverse)
    weight_term(2, x_turned, lambda p: grad_v[p], terms)
    to_plane(2, terms, got_plane, plane_send.at[2], plane_recv.at[2])

    drain(far_d, recv.at[7])
    fill_rows(delta_rows, deltas, far_d)

    def reverse_grad(p, half, h):
        grad_score = (prob_t[h] * (grad_prob_t[h] - delta_rows[h])).astype(BF16)
        merge(grad_k, p, half, nn(grad_score, q_all[p]).astype(BF16))

    heads(reverse_grad)
    weight_term(1, x_turned, lambda p: grad_k[p], terms)
    to_plane(1, terms, got_plane, plane_send.at[1], plane_recv.at[1])

    for m in (0, 3, 2):
        to_line(m, terms, got_plane, sum_plane, got_line, plane_recv.at[m], send.at[8], recv.at[8])
    nodes = jnp.zeros((256, 512), F32)
    for grad, w in ((grad_q, wq), (grad_v, wv), (grad_k, wk)):
        joined = jnp.concatenate([grad[p] for p in range(4)], axis=1)
        nodes = nodes + nt(joined, w[...])
    grad_nodes[...] = nodes.astype(BF16)
    to_line(1, terms, got_plane, sum_plane, got_line, plane_recv.at[1], send.at[8], recv.at[8])
    drain(got_line, recv.at[8])
    acc = got_line[0].astype(F32)
    for i in range(1, 8):
        acc = acc + got_line[i].astype(F32)
    result[...] = jnp.where(lax.rem(zpos, 2) == 0, acc[:, :64], acc[:, 64:])

    for k, ref in enumerate((held_x, held_g, held_l)):
        drain(ref.at[pl.ds(0, DEVICES - 1)], send.at[k])
    for k, ref in enumerate((far_x, far_g)):
        drain(ref.at[pl.ds(0, PIECES - 1)], send.at[3 + k])
    drain(far_l.at[pl.ds(0, 15)], send.at[5])
    drain(held_d.at[pl.ds(0, DEVICES - 1)], send.at[6])
    drain(far_d.at[pl.ds(0, 15)], send.at[7])
    for m in range(4):
        drain(got_plane.at[m, pl.ds(1, 31)], plane_send.at[m])
    drain(got_line.at[pl.ds(0, 7)], send.at[8])


def vmem(count):
    return [pl.BlockSpec(memory_space=pltpu.VMEM)] * count


def sds(shape, kind):
    return jax.ShapeDtypeStruct(shape, kind)


def params(cid=None):
    if cid is None:
        return pltpu.CompilerParams(vmem_limit_bytes=LIMIT)
    return pltpu.CompilerParams(vmem_limit_bytes=LIMIT, collective_id=cid, has_side_effects=True)


def on_device(x, g, lse, wq, wk, wv, wo, partners):
    smem = pl.BlockSpec(memory_space=pltpu.SMEM)
    dma = pltpu.SemaphoreType.DMA
    regular = pltpu.SemaphoreType.REGULAR
    wide = pltpu.VMEM((PIECES, 3, 8, 128), BF16)
    small = pltpu.VMEM((16, 3, 1, 128), F32)
    held = pltpu.VMEM((DEVICES, 8, 128), BF16)
    held_small = pltpu.VMEM((DEVICES, 1, 128), F32)
    cut = pltpu.VMEM((PIECES, 8, 128), BF16)
    cut_small = pltpu.VMEM((16, 1, 128), F32)
    split = pltpu.VMEM((4, 1024, 128), BF16)
    square = pltpu.VMEM((8, 256, 1024), F32)
    part = pltpu.VMEM((8, 256, 128), F32)
    joined = pltpu.VMEM((4, 256, 128), BF16)
    column = pltpu.VMEM((8, 256, 1), F32)
    row = pltpu.VMEM((8, 1, 1024), F32)
    return pl.pallas_call(
        whole_kernel,
        out_shape=(sds((256, 512), BF16), sds((64, 64), F32)),
        in_specs=[smem] + vmem(7),
        out_specs=tuple(vmem(2)),
        scratch_shapes=[
            cut, cut, cut_small, held, held, held_small, held_small, wide, wide, small, small,
            wide, wide, small, small,
            split, split, split, split, square, square, square, square,
            part, joined, joined, joined, joined, part, cut_small,
            column, column, row, row,
            pltpu.VMEM((4, 2, 4, 4, 64, 128), BF16), pltpu.VMEM((4, 32, 64, 128), BF16),
            pltpu.VMEM((4, 64, 128), BF16), pltpu.VMEM((8, 64, 128), BF16),
            regular, regular, dma((9,)), dma((9,)), dma((4,)), dma((4,)),
        ],
        compiler_params=params(0),
        name="whole",
    )(partners, x, g, lse, wq, wk, wv, wo)


def solution(mesh):
    return jax.shard_map(
        on_device,
        mesh=mesh,
        in_specs=(
            P(("gx", "gy"), None),
            P(("gx", "gy"), None),
            P(None, ("gx", "gy")),
            P(),
            P(),
            P(),
            P(),
            P(),
        ),
        out_specs=(P(("gx", "gy"), None), P("gx", "gy")),
        check_vma=False,
    )
```

```python
import functools

import jax
import jax.numpy as jnp
from jax import lax
from jax.experimental import pallas as pl
from jax.experimental.pallas import tpu as pltpu
from jax.sharding import PartitionSpec as P

MESH = pl.DeviceIdType.MESH
F32 = jnp.float32
BF16 = jnp.bfloat16
DEVICES = 256
PIECES = 128
LIMIT = 60 * 1024 * 1024


def nt(a, b):
    return lax.dot_general(a, b, (((1,), (1,)), ((), ())), preferred_element_type=F32)


def nn(a, b):
    return lax.dot_general(a, b, (((1,), (0,)), ((), ())), preferred_element_type=F32)


def position():
    gx = lax.axis_index("gx")
    gy = lax.axis_index("gy")
    x = lax.rem(gx, 4)
    y = lax.rem(lax.div(gy, 2), 4)
    z = lax.div(gx, 4) + 2 * lax.div(gy, 8)
    core = lax.rem(gy, 2)
    return x, y, z, core


def place(x, y, z, core):
    return lax.rem(z, 2) * 4 + x, (lax.div(z, 2) * 4 + y) * 2 + core


def rendezvous(barrier, second, third):
    x, y, z, core = position()

    def wide(i):
        return place(lax.rem(x + lax.rem(i, 4), 4), y, z, lax.rem(core + lax.div(i, 4), 2))

    def signal(sem, peer):
        pl.semaphore_signal(sem, inc=1, device_id=peer, device_id_type=MESH)

    def first():
        for i in (4, 2, 6, 3, 5, 1, 7):
            signal(barrier, place(x, y, lax.rem(z + i, 8), core))
        for i in (2, 1, 3):
            signal(barrier, place(x, lax.rem(y + i, 4), z, core))
        for i in range(1, 8):
            signal(barrier, wide(i))

    def rest():
        pl.semaphore_wait(barrier, 17)
        for i in range(1, 8):
            signal(second, wide(i))
        pl.semaphore_wait(second, 7)
        for i in range(1, 4):
            signal(third, place(x, lax.rem(y + i, 4), z, core))
        pl.semaphore_wait(third, 3)

    return first, rest


def spread(src_of, dst, gx, gy, send_sem, recv_sem):
    me = gx * 32 + gy
    group = lax.div(gy, 8)
    inner = lax.rem(gy, 8)

    def send(tx, b, k):
        pltpu.make_async_remote_copy(
            src_ref=src_of(tx, b, k),
            dst_ref=dst.at[me],
            send_sem=send_sem,
            recv_sem=recv_sem,
            device_id=(tx, 8 * b + k),
            device_id_type=MESH,
        ).start()

    def octet(i, carry):
        tx = lax.rem(gx + lax.div(i, 4), 8)
        b = lax.rem(group + lax.rem(i, 4), 4)
        for k in range(8):
            send(tx, b, k)
        return carry

    lax.fori_loop(1, 32, octet, 0)
    for k in range(1, 8):
        send(gx, group, lax.rem(inner + k, 8))
    pltpu.make_async_copy(src_of(gx, group, inner), dst.at[me], recv_sem).start()


def drain(ref, sem):
    pltpu.make_async_copy(ref, ref, sem).wait()


def piece_of(tx, b, k):
    return tx * 16 + 8 * lax.rem(b, 2) + k


def small_of(tx, b, k):
    return (lax.div(tx, 4) * 2 + lax.rem(tx, 2)) * 4 + (k % 4 if isinstance(k, int) else lax.rem(k, 4))


def wide_octet(a):
    x, y, z, core = position()
    tz = lax.rem(z + lax.rem(lax.div(a, 4) + 1 + core, 4) + 7 - core, 8)
    tx = lax.rem(tz, 2) * 4 + lax.rem(x + lax.rem(a, 4), 4)
    return tx, lax.div(tz, 2)


def choose_wide(partners_ref, held, chosen):
    def octet(a, carry):
        tx, b = wide_octet(a)
        block = tx * 32 + 8 * b
        for k in range(8):
            for j in range(3):
                chosen[8 * a + k, j] = held[partners_ref[j, block + k]]
        return carry

    lax.fori_loop(0, 16, octet, 0)


def deliver_wide(slot, chosen, dst, send_sem, recv_sem):
    inner = lax.rem(lax.axis_index("gy"), 8)

    def send(a, tx, b, k):
        pltpu.make_async_remote_copy(
            src_ref=chosen.at[8 * a + k],
            dst_ref=dst.at[slot],
            send_sem=send_sem,
            recv_sem=recv_sem,
            device_id=(tx, 8 * b + k),
            device_id_type=MESH,
        ).start()

    def octet(a, carry):
        tx, b = wide_octet(a)
        for k in range(8):
            send(a, tx, b, k)
        return carry

    lax.fori_loop(1, 16, octet, 0)
    tx, b = wide_octet(0)
    for k in range(1, 8):
        send(0, tx, b, lax.rem(inner + k, 8))
    pltpu.make_async_copy(chosen.at[inner], dst.at[slot], recv_sem).start()


def small_target(index):
    x, y, z, core = position()
    tx = lax.div(x, 2) * 2 + lax.rem(x + lax.rem(index, 2), 2)
    ty = lax.div(y, 2) * 2 + lax.rem(y + lax.rem(lax.div(index, 2), 2), 2)
    tz = lax.div(z, 2) * 2 + lax.rem(z + lax.rem(lax.div(index, 4), 2), 2)
    tc = lax.rem(core + lax.div(index, 8), 2)
    return place(tx, ty, tz, tc)


def choose(target, count, partners_ref, held, chosen):
    def pick(index, carry):
        tx, ty = target(index)
        block = tx * 32 + ty
        for j in range(3):
            chosen[index, j] = held[partners_ref[j, block]]
        return carry

    lax.fori_loop(0, count, pick, 0)


def deliver(target, count, self_index, slot, chosen, dst, send_sem, recv_sem):
    def send(index, carry):
        tx, ty = target(index)
        pltpu.make_async_remote_copy(
            src_ref=chosen.at[index],
            dst_ref=dst.at[slot],
            send_sem=send_sem,
            recv_sem=recv_sem,
            device_id=(tx, ty),
            device_id_type=MESH,
        ).start()
        return carry

    lax.fori_loop(0, self_index, send, 0)
    lax.fori_loop(self_index + 1, count, send, 0)
    pltpu.make_async_copy(chosen.at[self_index], dst.at[slot], recv_sem).start()


def project(w, src, dst, rows, scale=None, transposed=False):
    full = nt(src, w[...]) if transposed else nn(src, w[...])
    low = full.astype(BF16)
    if scale is not None:
        low = low * jnp.asarray(scale, BF16)
    for p in range(4):
        dst[p, rows, :] = low[:, 128 * p : 128 * (p + 1)]


def unpack(far, j):
    return jnp.concatenate([far[32 * c : 32 * (c + 1), j].reshape(256, 128) for c in range(4)], axis=1)


def half_mask(half):
    lane = lax.broadcasted_iota(jnp.int32, (1, 128), 1)
    return (lane < 64) if half == 0 else (lane >= 64)


def fill_rows(dst, own, far):
    for h in range(8):
        for half in range(2):
            dst[h, :, 128 * half : 128 * (half + 1)] = own[2 * h + half]
            for j in range(3):
                lo = 256 * (j + 1) + 128 * half
                dst[h, :, lo : lo + 128] = far[2 * h + half, j]


def heads(body):
    def pair(p, carry):
        for half in range(2):
            body(p, half, 2 * p + half)
        return carry

    lax.fori_loop(0, 4, pair, 0)


def own_part(ref, p, half):
    return jnp.where(half_mask(half), ref[p, 0:256, :], jnp.zeros((), BF16))


def merge(dst, p, half, value):
    if half == 0:
        dst[p] = value
    else:
        dst[p] = jnp.where(half_mask(0), dst[p], value)


def join(ref):
    return jnp.concatenate([ref[p] for p in range(4)], axis=1)


def turn_rows(ref):
    return jnp.transpose(join(ref), (1, 0))


def weight_term(m, left, right_of, terms):
    first = half_mask(0)
    for q in range(2):
        full = nn(left, jnp.concatenate([right_of(2 * q), right_of(2 * q + 1)], axis=1))
        for r in range(2):
            low = full[:256, 128 * r : 128 * (r + 1)]
            high = full[256:, 128 * r : 128 * (r + 1)]
            even = jnp.where(first, low, pltpu.roll(high, 64, 1))
            odd = jnp.where(first, pltpu.roll(low, 64, 1), high)
            terms[m, 0, 2 * q + r] = even.astype(BF16).reshape(4, 64, 128)
            terms[m, 1, 2 * q + r] = odd.astype(BF16).reshape(4, 64, 128)


def core_copy(m, terms, got_core, send_sem, recv_sem):
    x, y, z, core = position()
    return pltpu.make_async_remote_copy(
        src_ref=terms.at[m, 1 - core],
        dst_ref=got_core.at[m],
        send_sem=send_sem,
        recv_sem=recv_sem,
        device_id=place(x, y, z, 1 - core),
        device_id_type=MESH,
    )


def to_plane(m, terms, got_core, sum_core, got_plane, core_send, core_recv, send_sem, recv_sem):
    x, y, z, core = position()
    core_copy(m, terms, got_core, core_send, core_recv).wait()
    for p in range(4):
        sum_core[m, p] = (terms[m, core, p].astype(F32) + got_core[m, p].astype(F32)).astype(BF16)

    def step(i, carry):
        tx = lax.rem(x + lax.rem(i, 4), 4)
        ty = lax.rem(y + lax.div(i, 4), 4)
        pltpu.make_async_remote_copy(
            src_ref=sum_core.at[m, ty, tx],
            dst_ref=got_plane.at[m, i],
            send_sem=send_sem,
            recv_sem=recv_sem,
            device_id=place(tx, ty, z, core),
            device_id_type=MESH,
        ).start()
        return carry

    lax.fori_loop(1, 16, step, 0)


def to_line(m, sum_core, got_plane, sum_plane, got_line, plane_sem, send_sem, recv_sem):
    x, y, z, core = position()
    drain(got_plane.at[m, pl.ds(1, 15)], plane_sem)

    total = sum_core[m, y, x].astype(F32)
    for i in range(1, 16):
        total = total + got_plane[m, i].astype(F32)
    sum_plane[m] = total.astype(BF16)
    for i in range(2):
        tz = 2 * m + i

        @pl.when(z != tz)
        def _():
            pltpu.make_async_remote_copy(
                src_ref=sum_plane.at[m],
                dst_ref=got_line.at[z],
                send_sem=send_sem,
                recv_sem=recv_sem,
                device_id=place(x, y, tz, core),
                device_id_type=MESH,
            ).start()

        @pl.when(z == tz)
        def _():
            pltpu.make_async_copy(sum_plane.at[m], got_line.at[z], recv_sem).start()


def whole_kernel(partners_ref, x_in, g_in, lse_in, wq_in, wk_in, wv_in, wo_in, nodes, result,
                 x, g, lse, wq, wk, wv, wo, load,
                 cut_x, cut_g, cut_l, held_x, held_g, held_l, held_d, pick_x, pick_g, pick_l, pick_d,
                 far_x, far_g, far_l, far_d,
                 q_all, k_all, v_all, d_all, prob, grad_prob, prob_t, grad_prob_t,
                 part_out, out, grad_q, grad_k, grad_v, part_v, deltas,
                 lse_cols, delta_cols, lse_rows, delta_rows,
                 terms, got_core, sum_core, got_plane, sum_plane, got_line,
                 second, third, send, recv, core_send, core_recv, plane_send, plane_recv):
    gx = lax.axis_index("gx")
    gy = lax.axis_index("gy")
    zpos = lax.div(gx, 4) + 2 * lax.div(gy, 8)
    core = lax.rem(gy, 2)
    first, rest = rendezvous(pltpu.get_barrier_semaphore(), second, third)
    loads = [
        pltpu.make_async_copy(src, dst, load.at[k])
        for k, (src, dst) in enumerate(
            zip((x_in, g_in, lse_in, wq_in, wk_in, wv_in, wo_in), (x, g, lse, wq, wk, wv, wo))
        )
    ]
    for copy in loads:
        copy.start()
    first()
    for copy in loads[:3]:
        copy.wait()
    for c in range(4):
        cut_x[32 * c : 32 * (c + 1)] = x[:, 128 * c : 128 * (c + 1)].reshape(32, 8, 128)
        cut_g[32 * c : 32 * (c + 1)] = g[:, 128 * c : 128 * (c + 1)].reshape(32, 8, 128)
    for h in range(8):
        for half in range(2):
            cut_l[2 * h + half] = lse[h : h + 1, 128 * half : 128 * (half + 1)]
    rest()
    spread(lambda tx, b, k: cut_x.at[piece_of(tx, b, k)], held_x, gx, gy, send.at[0], recv.at[0])
    spread(lambda tx, b, k: cut_g.at[piece_of(tx, b, k)], held_g, gx, gy, send.at[1], recv.at[1])
    spread(lambda tx, b, k: cut_l.at[small_of(tx, b, k)], held_l, gx, gy, send.at[2], recv.at[2])

    for copy in loads[3:]:
        copy.wait()
    own = pl.ds(0, 256)
    project(wq, x[...], q_all, own, scale=0.125)
    project(wk, x[...], k_all, own)
    project(wv, x[...], v_all, own)
    project(wo, g[...], d_all, own, transposed=True)
    turned = jnp.transpose(lse[...], (1, 0))
    for h in range(8):
        lse_cols[h] = turned[:, h : h + 1]

    group = lax.div(gy, 8)
    inner = lax.rem(gy, 8)
    slot = piece_of(gx, group, inner)
    small_slot = small_of(gx, group, inner)
    drain(held_x, recv.at[0])
    choose_wide(partners_ref, held_x, pick_x)
    deliver_wide(slot, pick_x, far_x, send.at[3], recv.at[3])

    def own_forward(p, half, h):
        score = nt(own_part(q_all, p, half), k_all[p, 0:256, :])
        prob[h, :, 0:256] = jnp.exp(jnp.minimum(score - lse_cols[h], 0.0))
        part_out[h] = nn(prob[h, :, 0:256].astype(BF16), v_all[p, 0:256, :])
        grad_prob[h, :, 0:256] = nt(own_part(d_all, p, half), v_all[p, 0:256, :])

    heads(own_forward)

    drain(held_g, recv.at[1])
    choose_wide(partners_ref, held_g, pick_g)
    deliver_wide(slot, pick_g, far_g, send.at[4], recv.at[4])
    drain(held_l, recv.at[2])
    choose(small_target, 16, partners_ref, held_l, pick_l)
    deliver(small_target, 16, 0, small_slot, pick_l, far_l, send.at[5], recv.at[5])

    def own_reverse(p, half, h):
        score = nt(own_part(k_all, p, half), q_all[p, 0:256, :])
        row = jnp.concatenate([cut_l[2 * h], cut_l[2 * h + 1]], axis=1)
        prob_t[h, :, 0:256] = jnp.exp(jnp.minimum(score - row, 0.0))
        part_v[h] = nn(prob_t[h, :, 0:256].astype(BF16), d_all[p, 0:256, :])
        grad_prob_t[h, :, 0:256] = nt(own_part(v_all, p, half), d_all[p, 0:256, :])

    heads(own_reverse)

    drain(far_x, recv.at[3])
    for j in range(3):
        rows = pl.ds(256 * (j + 1), 256)
        src = unpack(far_x, j)
        project(wk, src, k_all, rows)
        project(wv, src, v_all, rows)
        project(wq, src, q_all, rows, scale=0.125)

    def forward(p, half, h):
        score = nt(own_part(q_all, p, half), k_all[p, 256:, :])
        prob[h, :, 256:] = jnp.exp(jnp.minimum(score - lse_cols[h], 0.0))
        low = (part_out[h] + nn(prob[h, :, 256:].astype(BF16), v_all[p, 256:, :])).astype(BF16)
        d_own = own_part(d_all, p, half)
        grad_prob[h, :, 256:] = nt(d_own, v_all[p, 256:, :])
        delta = jnp.sum(d_own.astype(F32) * low.astype(F32), axis=1, keepdims=True)
        delta_cols[h] = delta
        merge(out, p, half, low)

    heads(forward)
    lane = lax.broadcasted_iota(jnp.int32, (256, 128), 1)
    flat = jnp.zeros((256, 128), F32)
    for h in range(8):
        flat = jnp.where(lane == h, delta_cols[h], flat)
    turned = jnp.transpose(flat, (1, 0))
    for h in range(8):
        for half in range(2):
            deltas[2 * h + half] = turned[h : h + 1, 128 * half : 128 * (half + 1)]
    spread(lambda tx, b, k: deltas.at[small_of(tx, b, k)], held_d, gx, gy, send.at[6], recv.at[6])

    def forward_grad(p, half, h):
        grad_score = (prob[h] * (grad_prob[h] - delta_cols[h])).astype(BF16)
        merge(grad_q, p, half, (nn(grad_score, k_all[p]) * 0.125).astype(BF16))

    heads(forward_grad)

    x_turned = jnp.transpose(x[...], (1, 0))
    weight_term(0, x_turned, lambda p: grad_q[p], terms)
    core_copy(0, terms, got_core, core_send.at[0], core_recv.at[0]).start()
    out_turned = turn_rows(out)
    weight_term(3, out_turned, lambda p: g[:, 128 * p : 128 * (p + 1)], terms)
    core_copy(3, terms, got_core, core_send.at[3], core_recv.at[3]).start()

    drain(held_d, recv.at[6])
    choose(small_target, 16, partners_ref, held_d, pick_d)
    deliver(small_target, 16, 0, small_slot, pick_d, far_d, send.at[7], recv.at[7])

    to_plane(0, terms, got_core, sum_core, got_plane, core_send.at[0], core_recv.at[0], plane_send.at[0], plane_recv.at[0])
    to_plane(3, terms, got_core, sum_core, got_plane, core_send.at[3], core_recv.at[3], plane_send.at[3], plane_recv.at[3])

    drain(far_g, recv.at[4])
    drain(far_l, recv.at[5])
    for j in range(3):
        project(wo, unpack(far_g, j), d_all, pl.ds(256 * (j + 1), 256), transposed=True)
    fill_rows(lse_rows, cut_l, far_l)

    def reverse(p, half, h):
        score = nt(own_part(k_all, p, half), q_all[p, 256:, :])
        prob_t[h, :, 256:] = jnp.exp(jnp.minimum(score - lse_rows[h, :, 256:], 0.0))
        low = (part_v[h] + nn(prob_t[h, :, 256:].astype(BF16), d_all[p, 256:, :])).astype(BF16)
        merge(grad_v, p, half, low)
        grad_prob_t[h, :, 256:] = nt(own_part(v_all, p, half), d_all[p, 256:, :])

    heads(reverse)
    weight_term(2, x_turned, lambda p: grad_v[p], terms)
    core_copy(2, terms, got_core, core_send.at[2], core_recv.at[2]).start()
    nodes[...] = nt(join(grad_q), wq[...]) + nt(join(grad_v), wv[...])

    drain(far_d, recv.at[7])
    fill_rows(delta_rows, deltas, far_d)

    def reverse_grad(p, half, h):
        grad_score = (prob_t[h] * (grad_prob_t[h] - delta_rows[h])).astype(BF16)
        merge(grad_k, p, half, nn(grad_score, q_all[p]).astype(BF16))

    heads(reverse_grad)
    to_plane(2, terms, got_core, sum_core, got_plane, core_send.at[2], core_recv.at[2], plane_send.at[2], plane_recv.at[2])
    weight_term(1, x_turned, lambda p: grad_k[p], terms)
    core_copy(1, terms, got_core, core_send.at[1], core_recv.at[1]).start()

    nodes[...] = nodes[...] + nt(join(grad_k), wk[...])
    to_plane(1, terms, got_core, sum_core, got_plane, core_send.at[1], core_recv.at[1], plane_send.at[1], plane_recv.at[1])
    for m in (0, 3, 2):
        to_line(m, sum_core, got_plane, sum_plane, got_line, plane_recv.at[m], send.at[8], recv.at[8])
    to_line(1, sum_core, got_plane, sum_plane, got_line, plane_recv.at[1], send.at[8], recv.at[8])
    drain(got_line, recv.at[8])
    acc = got_line[0].astype(F32)
    for i in range(1, 8):
        acc = acc + got_line[i].astype(F32)
    result[...] = jnp.where(lax.rem(zpos, 2) == 0, acc[:, :64], acc[:, 64:])

    for k, ref in enumerate((held_x, held_g, held_l)):
        drain(ref.at[pl.ds(0, DEVICES - 1)], send.at[k])
    for k, ref in enumerate((far_x, far_g)):
        drain(ref.at[pl.ds(0, PIECES - 1)], send.at[3 + k])
    drain(far_l.at[pl.ds(0, 15)], send.at[5])
    drain(held_d.at[pl.ds(0, DEVICES - 1)], send.at[6])
    drain(far_d.at[pl.ds(0, 15)], send.at[7])
    for m in range(4):
        drain(got_plane.at[m, pl.ds(1, 15)], plane_send.at[m])
    drain(got_line.at[pl.ds(0, 7)], send.at[8])


def vmem(count):
    return [pl.BlockSpec(memory_space=pltpu.VMEM)] * count


def sds(shape, kind):
    return jax.ShapeDtypeStruct(shape, kind)


def params(cid=None):
    if cid is None:
        return pltpu.CompilerParams(vmem_limit_bytes=LIMIT)
    return pltpu.CompilerParams(vmem_limit_bytes=LIMIT, collective_id=cid, has_side_effects=True)


def on_device(x, g, lse, wq, wk, wv, wo, partners):
    smem = pl.BlockSpec(memory_space=pltpu.SMEM)
    dma = pltpu.SemaphoreType.DMA
    regular = pltpu.SemaphoreType.REGULAR
    wide = pltpu.VMEM((PIECES, 3, 8, 128), BF16)
    small = pltpu.VMEM((16, 3, 1, 128), F32)
    held = pltpu.VMEM((DEVICES, 8, 128), BF16)
    held_small = pltpu.VMEM((DEVICES, 1, 128), F32)
    cut = pltpu.VMEM((PIECES, 8, 128), BF16)
    cut_small = pltpu.VMEM((16, 1, 128), F32)
    split = pltpu.VMEM((4, 1024, 128), BF16)
    square = pltpu.VMEM((8, 256, 1024), F32)
    part = pltpu.VMEM((8, 256, 128), F32)
    joined = pltpu.VMEM((4, 256, 128), BF16)
    column = pltpu.VMEM((8, 256, 1), F32)
    row = pltpu.VMEM((8, 1, 1024), F32)
    rows = pltpu.VMEM((256, 512), BF16)
    weight = pltpu.VMEM((512, 512), BF16)
    tiles = pltpu.VMEM((4, 4, 4, 64, 128), BF16)
    nodes, result = pl.pallas_call(
        whole_kernel,
        out_shape=(sds((256, 512), F32), sds((64, 64), F32)),
        in_specs=[smem] + [pl.BlockSpec(memory_space=pl.ANY)] * 7,
        out_specs=tuple(vmem(2)),
        scratch_shapes=[
            rows, rows, pltpu.VMEM((8, 256), F32), weight, weight, weight, weight, dma((7,)),
            cut, cut, cut_small, held, held, held_small, held_small, wide, wide, small, small,
            wide, wide, small, small,
            split, split, split, split, square, square, square, square,
            part, joined, joined, joined, joined, part, cut_small,
            column, column, row, row,
            pltpu.VMEM((4, 2, 4, 4, 64, 128), BF16), tiles, tiles, pltpu.VMEM((4, 16, 64, 128), BF16),
            pltpu.VMEM((4, 64, 128), BF16), pltpu.VMEM((8, 64, 128), BF16),
            regular, regular, dma((9,)), dma((9,)), dma((4,)), dma((4,)), dma((4,)), dma((4,)),
        ],
        compiler_params=params(0),
        name="whole",
    )(partners.T, x, g, lse, wq, wk, wv, wo)
    return nodes.astype(BF16), result


def solution(mesh):
    return jax.shard_map(
        on_device,
        mesh=mesh,
        in_specs=(
            P(("gx", "gy"), None),
            P(("gx", "gy"), None),
            P(None, ("gx", "gy")),
            P(),
            P(),
            P(),
            P(),
            P(),
        ),
        out_specs=(P(("gx", "gy"), None), P("gx", "gy")),
        check_vma=False,
    )
```

```python
import functools

import jax
import jax.numpy as jnp
from jax import lax
from jax.experimental import pallas as pl
from jax.experimental.pallas import tpu as pltpu
from jax.sharding import PartitionSpec as P

MESH = pl.DeviceIdType.MESH
F32 = jnp.float32
BF16 = jnp.bfloat16
DEVICES = 256
PIECES = 128
SPLIT = 16
EARLY = 6
LIMIT = 50 * 1024 * 1024


def nt(a, b):
    return lax.dot_general(a, b, (((1,), (1,)), ((), ())), preferred_element_type=F32)


def nn(a, b):
    return lax.dot_general(a, b, (((1,), (0,)), ((), ())), preferred_element_type=F32)


def position():
    gx = lax.axis_index("gx")
    gy = lax.axis_index("gy")
    x = lax.rem(gx, 4)
    y = lax.rem(lax.div(gy, 2), 4)
    z = lax.div(gx, 4) + 2 * lax.div(gy, 8)
    core = lax.rem(gy, 2)
    return x, y, z, core


def place(x, y, z, core):
    return lax.rem(z, 2) * 4 + x, (lax.div(z, 2) * 4 + y) * 2 + core


def rendezvous(barrier, second):
    x, y, z, core = position()

    def signal(sem, peer):
        pl.semaphore_signal(sem, inc=1, device_id=peer, device_id_type=MESH)

    def line(sem):
        for i in (4, 3, 5, 2, 6, 1, 7):
            signal(sem, place(x, y, lax.rem(z + i, 8), core))

    def first():
        line(barrier)
        for dy in (2, 1, 3, 0):
            for dx in (2, 1, 3, 0):
                for dc in (1, 0):
                    if dx or dy or dc:
                        signal(barrier, place(lax.rem(x + dx, 4), lax.rem(y + dy, 4), z, lax.rem(core + dc, 2)))

    def rest():
        pl.semaphore_wait(barrier, 38)
        line(second)
        pl.semaphore_wait(second, 7)

    return first, rest


def spread(src_of, dst, gx, gy, send_sem, recv_sem, lo=0, hi=32):
    me = gx * 32 + gy
    group = lax.div(gy, 8)
    inner = lax.rem(gy, 8)

    def send(tx, b, k):
        pltpu.make_async_remote_copy(
            src_ref=src_of(tx, b, k),
            dst_ref=dst.at[me],
            send_sem=send_sem,
            recv_sem=recv_sem,
            device_id=(tx, 8 * b + k),
            device_id_type=MESH,
        ).start()

    def octet(i, carry):
        tx = lax.rem(gx + lax.div(i, 4), 8)
        b = lax.rem(group + lax.rem(i, 4), 4)
        for k in range(8):
            send(tx, b, k)
        return carry

    lax.fori_loop(max(lo, 1), hi, octet, 0)
    if lo == 0:
        for k in range(1, 8):
            send(gx, group, lax.rem(inner + k, 8))
        pltpu.make_async_copy(src_of(gx, group, inner), dst.at[me], recv_sem).start()


def drain(ref, sem):
    pltpu.make_async_copy(ref, ref, sem).wait()


def piece_of(tx, b, k):
    return tx * 16 + 8 * lax.rem(b, 2) + k


def small_of(tx, b, k):
    return (lax.div(tx, 4) * 2 + lax.rem(tx, 2)) * 4 + (k % 4 if isinstance(k, int) else lax.rem(k, 4))


def wide_octet(a):
    x, y, z, core = position()
    tz = lax.rem(z + lax.rem(lax.div(a, 4) + 1 + core, 4) + 7 - core, 8)
    tx = lax.rem(tz, 2) * 4 + lax.rem(x + lax.rem(a, 4), 4)
    return tx, lax.div(tz, 2)


def choose_wide(partners_ref, held, chosen):
    def octet(a, carry):
        tx, b = wide_octet(a)
        block = tx * 32 + 8 * b
        for k in range(8):
            for j in range(3):
                chosen[8 * a + k, j] = held[partners_ref[j, block + k]]
        return carry

    lax.fori_loop(0, 16, octet, 0)


def deliver_wide(slot, chosen, dst, send_sem, early_sem, late_sem):
    inner = lax.rem(lax.axis_index("gy"), 8)

    def send(a, tx, b, k, recv_sem):
        pltpu.make_async_remote_copy(
            src_ref=chosen.at[8 * a + k],
            dst_ref=dst.at[slot],
            send_sem=send_sem,
            recv_sem=recv_sem,
            device_id=(tx, 8 * b + k),
            device_id_type=MESH,
        ).start()

    def octets(lo, hi, recv_sem):
        def octet(a, carry):
            tx, b = wide_octet(a)
            for k in range(8):
                send(a, tx, b, k, recv_sem)
            return carry

        lax.fori_loop(lo, hi, octet, 0)

    octets(1, EARLY, early_sem)
    tx, b = wide_octet(0)
    for k in range(1, 8):
        send(0, tx, b, lax.rem(inner + k, 8), early_sem)
    pltpu.make_async_copy(chosen.at[inner], dst.at[slot], early_sem).start()
    octets(EARLY, 16, late_sem)


def small_target(index):
    x, y, z, core = position()
    tx = lax.div(x, 2) * 2 + lax.rem(x + lax.rem(index, 2), 2)
    ty = lax.div(y, 2) * 2 + lax.rem(y + lax.rem(lax.div(index, 2), 2), 2)
    tz = lax.div(z, 4) * 4 + lax.rem(z + lax.rem(lax.div(index, 4), 4), 4)
    tc = lax.rem(core + lax.div(index, 16), 2)
    return place(tx, ty, tz, tc)


def spread_small(src, dst, gx, gy, send_sem, recv_sem):
    me = gx * 32 + gy
    group = lax.div(gy, 8)
    inner = lax.rem(gy, 8)

    def send(tx, b, k):
        pltpu.make_async_remote_copy(
            src_ref=src.at[small_of(tx, b, k)],
            dst_ref=dst.at[me],
            send_sem=send_sem,
            recv_sem=recv_sem,
            device_id=(tx, 8 * b + k),
            device_id_type=MESH,
        ).start()

    def octet(i, carry):
        tx = lax.rem(gx + lax.div(i, 2), 8)
        b = 2 * lax.rem(i, 2)
        for k in range(8):
            send(tx, b, k)
        return carry

    lax.fori_loop(2, 16, octet, 0)
    for b in (0, 2):

        @pl.when(group != b)
        def _():
            for k in range(8):
                send(gx, b, k)

        @pl.when(group == b)
        def _():
            for k in range(1, 8):
                send(gx, b, lax.rem(inner + k, 8))
            pltpu.make_async_copy(src.at[small_of(gx, b, inner)], dst.at[me], recv_sem).start()


def pass_small(partners_ref, held, chosen, dst, slot, send_sem, held_sem, recv_sem):
    drain(held, held_sem)

    def pick(index, carry):
        tx, ty = small_target(index)
        block = tx * 32 + ty
        for j in range(3):
            chosen[index, j] = held[partners_ref[j, block]]
        return carry

    lax.fori_loop(0, 32, pick, 0)

    def send(index, carry):
        tx, ty = small_target(index)
        pltpu.make_async_remote_copy(
            src_ref=chosen.at[index],
            dst_ref=dst.at[slot],
            send_sem=send_sem,
            recv_sem=recv_sem,
            device_id=(tx, ty),
            device_id_type=MESH,
        ).start()
        return carry

    lax.fori_loop(1, 32, send, 0)
    pltpu.make_async_copy(chosen.at[0], dst.at[slot], recv_sem).start()


def cube_target(index):
    x, y, z, core = position()
    tx = lax.div(x, 2) * 2 + lax.rem(x + lax.rem(index, 2), 2)
    ty = lax.div(y, 2) * 2 + lax.rem(y + lax.rem(lax.div(index, 2), 2), 2)
    tz = lax.div(z, 2) * 2 + lax.rem(z + lax.rem(lax.div(index, 4), 2), 2)
    tc = lax.rem(core + lax.div(index, 8), 2)
    return place(tx, ty, tz, tc)


def choose(target, count, partners_ref, held, chosen):
    def pick(index, carry):
        tx, ty = target(index)
        block = tx * 32 + ty
        for j in range(3):
            chosen[index, j] = held[partners_ref[j, block]]
        return carry

    lax.fori_loop(0, count, pick, 0)


def deliver(target, count, self_index, slot, chosen, dst, send_sem, recv_sem):
    def send(index, carry):
        tx, ty = target(index)
        pltpu.make_async_remote_copy(
            src_ref=chosen.at[index],
            dst_ref=dst.at[slot],
            send_sem=send_sem,
            recv_sem=recv_sem,
            device_id=(tx, ty),
            device_id_type=MESH,
        ).start()
        return carry

    lax.fori_loop(0, self_index, send, 0)
    lax.fori_loop(self_index + 1, count, send, 0)
    pltpu.make_async_copy(chosen.at[self_index], dst.at[slot], recv_sem).start()


def project(w, src, dst, rows, scale=None, transposed=False):
    full = nt(src, w[...]) if transposed else nn(src, w[...])
    low = full.astype(BF16)
    if scale is not None:
        low = low * jnp.asarray(scale, BF16)
    for p in range(4):
        dst[p, rows, :] = low[:, 128 * p : 128 * (p + 1)]


def unpack(far, j):
    return jnp.concatenate([far[32 * c : 32 * (c + 1), j].reshape(256, 128) for c in range(4)], axis=1)


def half_mask(half):
    lane = lax.broadcasted_iota(jnp.int32, (1, 128), 1)
    return (lane < 64) if half == 0 else (lane >= 64)


def fill_rows(dst, own, far):
    for h in range(8):
        for half in range(2):
            dst[h, :, 128 * half : 128 * (half + 1)] = own[2 * h + half]
            for j in range(3):
                lo = 256 * (j + 1) + 128 * half
                dst[h, :, lo : lo + 128] = far[2 * h + half, j]


def heads(body, lo=0, hi=4):
    def pair(p, carry):
        for half in range(2):
            body(p, half, 2 * p + half)
        return carry

    lax.fori_loop(lo, hi, pair, 0)


def own_part(ref, p, half):
    return jnp.where(half_mask(half), ref[p, 0:256, :], jnp.zeros((), BF16))


def merge(dst, p, half, value):
    if half == 0:
        dst[p] = value
    else:
        dst[p] = jnp.where(half_mask(0), dst[p], value)


def join(ref):
    return jnp.concatenate([ref[p] for p in range(4)], axis=1)


def turn_rows(ref):
    return jnp.transpose(join(ref), (1, 0))


def weight_term(m, left, right_of, terms):
    first = half_mask(0)
    for q in range(2):
        full = nn(left, jnp.concatenate([right_of(2 * q), right_of(2 * q + 1)], axis=1))
        for r in range(2):
            low = full[:256, 128 * r : 128 * (r + 1)]
            high = full[256:, 128 * r : 128 * (r + 1)]
            even = jnp.where(first, low, pltpu.roll(high, 64, 1))
            odd = jnp.where(first, pltpu.roll(low, 64, 1), high)
            terms[m, 0, 2 * q + r] = even.astype(BF16).reshape(4, 64, 128)
            terms[m, 1, 2 * q + r] = odd.astype(BF16).reshape(4, 64, 128)


def core_copy(m, terms, got_core, send_sem, recv_sem):
    x, y, z, core = position()
    return pltpu.make_async_remote_copy(
        src_ref=terms.at[m, 1 - core],
        dst_ref=got_core.at[m],
        send_sem=send_sem,
        recv_sem=recv_sem,
        device_id=place(x, y, z, 1 - core),
        device_id_type=MESH,
    )


def to_plane(m, terms, got_core, sum_core, got_plane, core_send, core_recv, send_sem, recv_sem):
    x, y, z, core = position()
    core_copy(m, terms, got_core, core_send, core_recv).wait()
    for p in range(4):
        sum_core[m, p] = (terms[m, core, p].astype(F32) + got_core[m, p].astype(F32)).astype(BF16)

    def step(i, carry):
        tx = lax.rem(x + lax.rem(i, 4), 4)
        ty = lax.rem(y + lax.div(i, 4), 4)
        pltpu.make_async_remote_copy(
            src_ref=sum_core.at[m, ty, tx],
            dst_ref=got_plane.at[m, i],
            send_sem=send_sem,
            recv_sem=recv_sem,
            device_id=place(tx, ty, z, core),
            device_id_type=MESH,
        ).start()
        return carry

    lax.fori_loop(1, 16, step, 0)


def to_line(m, sum_core, got_plane, sum_plane, got_line, plane_sem, send_sem, recv_sem):
    x, y, z, core = position()
    drain(got_plane.at[m, pl.ds(1, 15)], plane_sem)

    total = sum_core[m, y, x].astype(F32)
    for i in range(1, 16):
        total = total + got_plane[m, i].astype(F32)
    sum_plane[m] = total.astype(BF16)
    for i in range(2):
        tz = 2 * m + i

        @pl.when(z != tz)
        def _():
            pltpu.make_async_remote_copy(
                src_ref=sum_plane.at[m],
                dst_ref=got_line.at[z],
                send_sem=send_sem,
                recv_sem=recv_sem,
                device_id=place(x, y, tz, core),
                device_id_type=MESH,
            ).start()

        @pl.when(z == tz)
        def _():
            pltpu.make_async_copy(sum_plane.at[m], got_line.at[z], recv_sem).start()


def whole_kernel(partners_ref, x_in, g_in, lse_in, wq_in, wk_in, wv_in, wo_in, nodes, result,
                 x, g, lse, wq, wk, wv, wo, load,
                 cut_x, cut_g, cut_l, held_x, held_g, held_l, held_d, pick_x, pick_g, pick_l, pick_d,
                 far_x, far_g, far_l, far_d,
                 q_all, k_all, v_all, d_all, prob, grad_prob, prob_t, grad_prob_t,
                 part_out, out, grad_q, grad_k, grad_v, part_v, deltas,
                 lse_cols, delta_cols, lse_rows, delta_rows,
                 terms, got_core, sum_core, got_plane, sum_plane, got_line,
                 second, late, send, recv, core_send, core_recv, plane_send, plane_recv):
    gx = lax.axis_index("gx")
    gy = lax.axis_index("gy")
    zpos = lax.div(gx, 4) + 2 * lax.div(gy, 8)
    core = lax.rem(gy, 2)
    first, rest = rendezvous(pltpu.get_barrier_semaphore(), second)
    loads = [
        pltpu.make_async_copy(src, dst, load.at[k])
        for k, (src, dst) in enumerate(
            zip((x_in, g_in, lse_in, wq_in, wk_in, wv_in, wo_in), (x, g, lse, wq, wk, wv, wo))
        )
    ]
    for copy in loads:
        copy.start()
    first()
    for copy in loads[:3]:
        copy.wait()
    for c in range(4):
        cut_x[32 * c : 32 * (c + 1)] = x[:, 128 * c : 128 * (c + 1)].reshape(32, 8, 128)
        cut_g[32 * c : 32 * (c + 1)] = g[:, 128 * c : 128 * (c + 1)].reshape(32, 8, 128)
    for h in range(8):
        for half in range(2):
            cut_l[2 * h + half] = lse[h : h + 1, 128 * half : 128 * (half + 1)]
    rest()
    spread(lambda tx, b, k: cut_x.at[piece_of(tx, b, k)], held_x, gx, gy, send.at[0], recv.at[0])
    for copy in loads[3:]:
        copy.wait()
    own = pl.ds(0, 256)
    project(wq, x[...], q_all, own, scale=0.125)
    project(wk, x[...], k_all, own)
    project(wv, x[...], v_all, own)
    project(wo, g[...], d_all, own, transposed=True)
    turned = jnp.transpose(lse[...], (1, 0))
    for h in range(8):
        lse_cols[h] = turned[:, h : h + 1]

    group = lax.div(gy, 8)
    inner = lax.rem(gy, 8)
    slot = piece_of(gx, group, inner)
    small_slot = small_of(gx, group, inner)
    def own_forward(p, half, h):
        score = nt(own_part(q_all, p, half), k_all[p, 0:256, :])
        prob[h, :, 0:256] = jnp.exp(jnp.minimum(score - lse_cols[h], 0.0))
        part_out[h] = nn(prob[h, :, 0:256].astype(BF16), v_all[p, 0:256, :])
        grad_prob[h, :, 0:256] = nt(own_part(d_all, p, half), v_all[p, 0:256, :])

    heads(own_forward)

    def own_reverse(p, half, h):
        score = nt(own_part(k_all, p, half), q_all[p, 0:256, :])
        row = jnp.concatenate([cut_l[2 * h], cut_l[2 * h + 1]], axis=1)
        prob_t[h] = jnp.exp(jnp.minimum(score - row, 0.0))
        part_v[h] = nn(prob_t[h].astype(BF16), d_all[p, 0:256, :])
        grad_prob_t[h] = nt(own_part(v_all, p, half), d_all[p, 0:256, :])

    heads(own_reverse)

    spread(lambda tx, b, k: cut_g.at[piece_of(tx, b, k)], held_g, gx, gy, send.at[1], recv.at[1], 0, SPLIT)
    spread_small(cut_l, held_l, gx, gy, send.at[2], recv.at[2])
    drain(held_x, recv.at[0])
    choose_wide(partners_ref, held_x, pick_x)
    deliver_wide(slot, pick_x, far_x, send.at[3], recv.at[3], late.at[0])

    drain(far_x.at[pl.ds(0, 8 * EARLY)], recv.at[3])
    spread(lambda tx, b, k: cut_g.at[piece_of(tx, b, k)], held_g, gx, gy, send.at[1], recv.at[1], SPLIT, 32)
    holder = lax.rem(group, 2) == 0

    @pl.when(holder)
    def _():
        pass_small(partners_ref, held_l, pick_l, far_l, small_slot, send.at[5], recv.at[2], recv.at[5])

    drain(far_x.at[pl.ds(0, 128 - 8 * EARLY)], late.at[0])
    for j in range(3):
        rows = pl.ds(256 * (j + 1), 256)
        src = unpack(far_x, j)
        project(wk, src, k_all, rows)
        project(wv, src, v_all, rows)
        project(wq, src, q_all, rows, scale=0.125)

    def forward(p, half, h):
        score = nt(own_part(q_all, p, half), k_all[p, 256:, :])
        prob[h, :, 256:] = jnp.exp(jnp.minimum(score - lse_cols[h], 0.0))
        low = (part_out[h] + nn(prob[h, :, 256:].astype(BF16), v_all[p, 256:, :])).astype(BF16)
        d_own = own_part(d_all, p, half)
        grad_prob[h, :, 256:] = nt(d_own, v_all[p, 256:, :])
        delta = jnp.sum(d_own.astype(F32) * low.astype(F32), axis=1, keepdims=True)
        delta_cols[h] = delta
        merge(out, p, half, low)

    heads(forward)
    lane = lax.broadcasted_iota(jnp.int32, (256, 128), 1)
    flat = jnp.zeros((256, 128), F32)
    for h in range(8):
        flat = jnp.where(lane == h, delta_cols[h], flat)
    turned = jnp.transpose(flat, (1, 0))
    for h in range(8):
        for half in range(2):
            deltas[2 * h + half] = turned[h : h + 1, 128 * half : 128 * (half + 1)]
    spread(lambda tx, b, k: deltas.at[small_of(tx, b, k)], held_d, gx, gy, send.at[6], recv.at[6])
    drain(held_g, recv.at[1])
    choose_wide(partners_ref, held_g, pick_g)
    deliver_wide(slot, pick_g, far_g, send.at[4], recv.at[4], late.at[1])
    def forward_grad(p, half, h):
        grad_score = (prob[h] * (grad_prob[h] - delta_cols[h])).astype(BF16)
        merge(grad_q, p, half, (nn(grad_score, k_all[p]) * 0.125).astype(BF16))

    heads(forward_grad)

    x_turned = jnp.transpose(x[...], (1, 0))
    weight_term(0, x_turned, lambda p: grad_q[p], terms)
    core_copy(0, terms, got_core, core_send.at[0], core_recv.at[0]).start()
    out_turned = turn_rows(out)
    weight_term(3, out_turned, lambda p: g[:, 128 * p : 128 * (p + 1)], terms)
    core_copy(3, terms, got_core, core_send.at[3], core_recv.at[3]).start()

    drain(far_l, recv.at[5])
    fill_rows(lse_rows, cut_l, far_l)
    def reverse_prob(p, half, h):
        score = nt(own_part(k_all, p, half), q_all[p, 256:, :])
        prob[h, :, 256:] = jnp.exp(jnp.minimum(score - lse_rows[h, :, 256:], 0.0))

    heads(reverse_prob)

    drain(held_d, recv.at[6])
    choose(cube_target, 16, partners_ref, held_d, pick_d)
    deliver(cube_target, 16, 0, small_slot, pick_d, far_d, send.at[7], recv.at[7])

    to_plane(0, terms, got_core, sum_core, got_plane, core_send.at[0], core_recv.at[0], plane_send.at[0], plane_recv.at[0])
    to_plane(3, terms, got_core, sum_core, got_plane, core_send.at[3], core_recv.at[3], plane_send.at[3], plane_recv.at[3])

    drain(far_g.at[pl.ds(0, 8 * EARLY)], recv.at[4])
    drain(far_g.at[pl.ds(0, 128 - 8 * EARLY)], late.at[1])
    for j in range(3):
        project(wo, unpack(far_g, j), d_all, pl.ds(256 * (j + 1), 256), transposed=True)

    def reverse_value(p, half, h):
        low = (part_v[h] + nn(prob[h, :, 256:].astype(BF16), d_all[p, 256:, :])).astype(BF16)
        merge(grad_v, p, half, low)

    heads(reverse_value)
    weight_term(2, x_turned, lambda p: grad_v[p], terms)
    core_copy(2, terms, got_core, core_send.at[2], core_recv.at[2]).start()

    def reverse_prob_grad(p, half, h):
        grad_prob[h, :, 256:] = nt(own_part(v_all, p, half), d_all[p, 256:, :])

    heads(reverse_prob_grad)
    to_plane(2, terms, got_core, sum_core, got_plane, core_send.at[2], core_recv.at[2], plane_send.at[2], plane_recv.at[2])
    drain(far_d, recv.at[7])
    fill_rows(delta_rows, deltas, far_d)
    def reverse_grad(p, half, h):
        near = (prob_t[h] * (grad_prob_t[h] - delta_rows[h, :, 0:256])).astype(BF16)
        far = (prob[h, :, 256:] * (grad_prob[h, :, 256:] - delta_rows[h, :, 256:])).astype(BF16)
        both = nn(near, q_all[p, 0:256, :]) + nn(far, q_all[p, 256:, :])
        merge(grad_k, p, half, both.astype(BF16))

    heads(reverse_grad)
    weight_term(1, x_turned, lambda p: grad_k[p], terms)
    core_copy(1, terms, got_core, core_send.at[1], core_recv.at[1]).start()

    nodes[...] = nt(join(grad_q), wq[...]) + nt(join(grad_v), wv[...]) + nt(join(grad_k), wk[...])
    to_plane(1, terms, got_core, sum_core, got_plane, core_send.at[1], core_recv.at[1], plane_send.at[1], plane_recv.at[1])
    for m in (0, 3, 2):
        to_line(m, sum_core, got_plane, sum_plane, got_line, plane_recv.at[m], send.at[8], recv.at[8])
    to_line(1, sum_core, got_plane, sum_plane, got_line, plane_recv.at[1], send.at[8], recv.at[8])
    drain(got_line, recv.at[8])
    acc = got_line[0].astype(F32)
    for i in range(1, 8):
        acc = acc + got_line[i].astype(F32)
    result[...] = jnp.where(lax.rem(zpos, 2) == 0, acc[:, :64], acc[:, 64:])

    drain(held_d.at[pl.ds(0, DEVICES - 1)], send.at[6])
    drain(far_d.at[pl.ds(0, 15)], send.at[7])
    for k, ref in enumerate((held_x, held_g)):
        drain(ref.at[pl.ds(0, DEVICES - 1)], send.at[k])
    for k, ref in enumerate((far_x, far_g)):
        drain(ref.at[pl.ds(0, PIECES - 1)], send.at[3 + k])

    @pl.when(holder)
    def _():
        drain(held_l.at[pl.ds(0, 127)], send.at[2])
        drain(pick_l.at[pl.ds(0, 31)], send.at[5])

    @pl.when(jnp.logical_not(holder))
    def _():
        drain(held_l.at[pl.ds(0, 128)], send.at[2])

    for m in range(4):
        drain(got_plane.at[m, pl.ds(1, 15)], plane_send.at[m])
    drain(got_line.at[pl.ds(0, 7)], send.at[8])


def vmem(count):
    return [pl.BlockSpec(memory_space=pltpu.VMEM)] * count


def sds(shape, kind):
    return jax.ShapeDtypeStruct(shape, kind)


def params(cid=None):
    if cid is None:
        return pltpu.CompilerParams(vmem_limit_bytes=LIMIT)
    return pltpu.CompilerParams(vmem_limit_bytes=LIMIT, collective_id=cid, has_side_effects=True)


def on_device(x, g, lse, wq, wk, wv, wo, partners):
    smem = pl.BlockSpec(memory_space=pltpu.SMEM)
    dma = pltpu.SemaphoreType.DMA
    regular = pltpu.SemaphoreType.REGULAR
    wide = pltpu.VMEM((PIECES, 3, 8, 128), BF16)
    small = pltpu.VMEM((16, 3, 1, 128), F32)
    held = pltpu.VMEM((DEVICES, 8, 128), BF16)
    held_small = pltpu.VMEM((DEVICES, 1, 128), F32)
    pick_small = pltpu.VMEM((32, 3, 1, 128), F32)
    cut = pltpu.VMEM((PIECES, 8, 128), BF16)
    cut_small = pltpu.VMEM((16, 1, 128), F32)
    split = pltpu.VMEM((4, 1024, 128), BF16)
    square = pltpu.VMEM((8, 256, 1024), F32)
    tile = pltpu.VMEM((8, 256, 256), F32)
    part = pltpu.VMEM((8, 256, 128), F32)
    joined = pltpu.VMEM((4, 256, 128), BF16)
    column = pltpu.VMEM((8, 256, 1), F32)
    row = pltpu.VMEM((8, 1, 1024), F32)
    rows = pltpu.VMEM((256, 512), BF16)
    weight = pltpu.VMEM((512, 512), BF16)
    tiles = pltpu.VMEM((4, 4, 4, 64, 128), BF16)
    nodes, result = pl.pallas_call(
        whole_kernel,
        out_shape=(sds((256, 512), F32), sds((64, 64), F32)),
        in_specs=[smem] + [pl.BlockSpec(memory_space=pltpu.HBM)] * 7,
        out_specs=tuple(vmem(2)),
        scratch_shapes=[
            rows, rows, pltpu.VMEM((8, 256), F32), weight, weight, weight, weight, dma((7,)),
            cut, cut, cut_small, held, held, held_small, held_small, wide, wide, pick_small, small,
            wide, wide, small, small,
            split, split, split, split, square, square, tile, tile,
            part, joined, joined, joined, joined, part, cut_small,
            column, column, row, row,
            pltpu.VMEM((4, 2, 4, 4, 64, 128), BF16), tiles, tiles, pltpu.VMEM((4, 16, 64, 128), BF16),
            pltpu.VMEM((4, 64, 128), BF16), pltpu.VMEM((8, 64, 128), BF16),
            regular, dma((2,)), dma((9,)), dma((9,)), dma((4,)), dma((4,)), dma((4,)), dma((4,)),
        ],
        compiler_params=params(0),
        name="whole",
    )(*(pltpu.with_memory_space_constraint(a, pltpu.HBM) for a in (partners.T, x, g, lse, wq, wk, wv, wo)))
    return nodes.astype(BF16), result


def solution(mesh):
    return jax.shard_map(
        on_device,
        mesh=mesh,
        in_specs=(
            P(("gx", "gy"), None),
            P(("gx", "gy"), None),
            P(None, ("gx", "gy")),
            P(),
            P(),
            P(),
            P(),
            P(),
        ),
        out_specs=(P(("gx", "gy"), None), P("gx", "gy")),
        check_vma=False,
    )
```

```python
import functools

import jax
import jax.numpy as jnp
from jax import lax
from jax.experimental import pallas as pl
from jax.experimental.pallas import tpu as pltpu
from jax.sharding import PartitionSpec as P

MESH = pl.DeviceIdType.MESH
F32 = jnp.float32
BF16 = jnp.bfloat16
DEVICES = 256
PIECES = 128
SPLIT = 16
EARLY = 8
LIMIT = 50 * 1024 * 1024


def nt(a, b):
    return lax.dot_general(a, b, (((1,), (1,)), ((), ())), preferred_element_type=F32)


def nn(a, b):
    return lax.dot_general(a, b, (((1,), (0,)), ((), ())), preferred_element_type=F32)


def position():
    gx = lax.axis_index("gx")
    gy = lax.axis_index("gy")
    x = lax.rem(gx, 4)
    y = lax.rem(lax.div(gy, 2), 4)
    z = lax.div(gx, 4) + 2 * lax.div(gy, 8)
    core = lax.rem(gy, 2)
    return x, y, z, core


def place(x, y, z, core):
    return lax.rem(z, 2) * 4 + x, (lax.div(z, 2) * 4 + y) * 2 + core


def rendezvous(barrier, second):
    x, y, z, core = position()

    def signal(sem, peer):
        pl.semaphore_signal(sem, inc=1, device_id=peer, device_id_type=MESH)

    def line(sem):
        for i in (4, 3, 5, 2, 6, 1, 7):
            signal(sem, place(x, y, lax.rem(z + i, 8), core))

    def first():
        line(barrier)
        for dy in (2, 1, 3, 0):
            for dx in (2, 1, 3, 0):
                for dc in (1, 0):
                    if dx or dy or dc:
                        signal(barrier, place(lax.rem(x + dx, 4), lax.rem(y + dy, 4), z, lax.rem(core + dc, 2)))

    def rest():
        pl.semaphore_wait(barrier, 38)
        line(second)
        pl.semaphore_wait(second, 7)

    return first, rest


def spread(src_of, dst, gx, gy, send_sem, recv_sem, lo=0, hi=32):
    me = gx * 32 + gy
    group = lax.div(gy, 8)
    inner = lax.rem(gy, 8)

    def send(tx, b, k):
        pltpu.make_async_remote_copy(
            src_ref=src_of(tx, b, k),
            dst_ref=dst.at[me],
            send_sem=send_sem,
            recv_sem=recv_sem,
            device_id=(tx, 8 * b + k),
            device_id_type=MESH,
        ).start()

    def octet(i, carry):
        tx = lax.rem(gx + lax.div(i, 4), 8)
        b = lax.rem(group + lax.rem(i, 4), 4)
        for k in range(8):
            send(tx, b, k)
        return carry

    lax.fori_loop(max(lo, 1), hi, octet, 0)
    if lo == 0:
        for k in range(1, 8):
            send(gx, group, lax.rem(inner + k, 8))
        pltpu.make_async_copy(src_of(gx, group, inner), dst.at[me], recv_sem).start()


def drain(ref, sem):
    pltpu.make_async_copy(ref, ref, sem).wait()


def piece_of(tx, b, k):
    return tx * 16 + 8 * lax.rem(b, 2) + k


def small_of(tx, b, k):
    return (lax.div(tx, 4) * 2 + lax.rem(tx, 2)) * 4 + (k % 4 if isinstance(k, int) else lax.rem(k, 4))


def wide_octet(a):
    x, y, z, core = position()
    tz = lax.rem(z + lax.rem(lax.div(a, 4) + 1 + core, 4) + 7 - core, 8)
    tx = lax.rem(tz, 2) * 4 + lax.rem(x + lax.rem(a, 4), 4)
    return tx, lax.div(tz, 2)


def choose_wide(partners_ref, held, chosen):
    def octet(a, carry):
        tx, b = wide_octet(a)
        block = tx * 32 + 8 * b
        for k in range(8):
            for j in range(3):
                chosen[8 * a + k, j] = held[partners_ref[j, block + k]]
        return carry

    lax.fori_loop(0, 16, octet, 0)


def deliver_wide(slot, chosen, dst, send_sem, early_sem, late_sem):
    inner = lax.rem(lax.axis_index("gy"), 8)

    def send(a, tx, b, k, recv_sem):
        pltpu.make_async_remote_copy(
            src_ref=chosen.at[8 * a + k],
            dst_ref=dst.at[slot],
            send_sem=send_sem,
            recv_sem=recv_sem,
            device_id=(tx, 8 * b + k),
            device_id_type=MESH,
        ).start()

    def octets(lo, hi, recv_sem):
        def octet(a, carry):
            tx, b = wide_octet(a)
            for k in range(8):
                send(a, tx, b, k, recv_sem)
            return carry

        lax.fori_loop(lo, hi, octet, 0)

    octets(1, EARLY, early_sem)
    tx, b = wide_octet(0)
    for k in range(1, 8):
        send(0, tx, b, lax.rem(inner + k, 8), early_sem)
    pltpu.make_async_copy(chosen.at[inner], dst.at[slot], early_sem).start()
    octets(EARLY, 16, late_sem)


def small_target(index):
    x, y, z, core = position()
    tx = lax.div(x, 2) * 2 + lax.rem(x + lax.rem(index, 2), 2)
    ty = lax.div(y, 2) * 2 + lax.rem(y + lax.rem(lax.div(index, 2), 2), 2)
    tz = lax.div(z, 4) * 4 + lax.rem(z + lax.rem(lax.div(index, 4), 4), 4)
    tc = lax.rem(core + lax.div(index, 16), 2)
    return place(tx, ty, tz, tc)


def spread_small(src, dst, gx, gy, send_sem, recv_sem):
    me = gx * 32 + gy
    group = lax.div(gy, 8)
    inner = lax.rem(gy, 8)

    def send(tx, b, k):
        pltpu.make_async_remote_copy(
            src_ref=src.at[small_of(tx, b, k)],
            dst_ref=dst.at[me],
            send_sem=send_sem,
            recv_sem=recv_sem,
            device_id=(tx, 8 * b + k),
            device_id_type=MESH,
        ).start()

    def octet(i, carry):
        tx = lax.rem(gx + lax.div(i, 2), 8)
        b = 2 * lax.rem(i, 2)
        for k in range(8):
            send(tx, b, k)
        return carry

    lax.fori_loop(2, 16, octet, 0)
    for b in (0, 2):

        @pl.when(group != b)
        def _():
            for k in range(8):
                send(gx, b, k)

        @pl.when(group == b)
        def _():
            for k in range(1, 8):
                send(gx, b, lax.rem(inner + k, 8))
            pltpu.make_async_copy(src.at[small_of(gx, b, inner)], dst.at[me], recv_sem).start()


def pass_small(partners_ref, held, chosen, dst, slot, send_sem, held_sem, recv_sem):
    drain(held, held_sem)

    def pick(index, carry):
        tx, ty = small_target(index)
        block = tx * 32 + ty
        for j in range(3):
            chosen[index, j] = held[partners_ref[j, block]]
        return carry

    lax.fori_loop(0, 32, pick, 0)

    def send(index, carry):
        tx, ty = small_target(index)
        pltpu.make_async_remote_copy(
            src_ref=chosen.at[index],
            dst_ref=dst.at[slot],
            send_sem=send_sem,
            recv_sem=recv_sem,
            device_id=(tx, ty),
            device_id_type=MESH,
        ).start()
        return carry

    lax.fori_loop(1, 32, send, 0)
    pltpu.make_async_copy(chosen.at[0], dst.at[slot], recv_sem).start()


def cube_target(index):
    x, y, z, core = position()
    tx = lax.div(x, 2) * 2 + lax.rem(x + lax.rem(index, 2), 2)
    ty = lax.div(y, 2) * 2 + lax.rem(y + lax.rem(lax.div(index, 2), 2), 2)
    tz = lax.div(z, 2) * 2 + lax.rem(z + lax.rem(lax.div(index, 4), 2), 2)
    tc = lax.rem(core + lax.div(index, 8), 2)
    return place(tx, ty, tz, tc)


def choose(target, count, partners_ref, held, chosen):
    def pick(index, carry):
        tx, ty = target(index)
        block = tx * 32 + ty
        for j in range(3):
            chosen[index, j] = held[partners_ref[j, block]]
        return carry

    lax.fori_loop(0, count, pick, 0)


def deliver(target, count, self_index, slot, chosen, dst, send_sem, recv_sem):
    def send(index, carry):
        tx, ty = target(index)
        pltpu.make_async_remote_copy(
            src_ref=chosen.at[index],
            dst_ref=dst.at[slot],
            send_sem=send_sem,
            recv_sem=recv_sem,
            device_id=(tx, ty),
            device_id_type=MESH,
        ).start()
        return carry

    lax.fori_loop(0, self_index, send, 0)
    lax.fori_loop(self_index + 1, count, send, 0)
    pltpu.make_async_copy(chosen.at[self_index], dst.at[slot], recv_sem).start()


def project(w, src, dst, rows, scale=None, transposed=False):
    full = nt(src, w[...]) if transposed else nn(src, w[...])
    low = full.astype(BF16)
    if scale is not None:
        low = low * jnp.asarray(scale, BF16)
    for p in range(4):
        dst[p, rows, :] = low[:, 128 * p : 128 * (p + 1)]


def unpack(far, j):
    return jnp.concatenate([far[32 * c : 32 * (c + 1), j].reshape(256, 128) for c in range(4)], axis=1)


def half_mask(half):
    lane = lax.broadcasted_iota(jnp.int32, (1, 128), 1)
    return (lane < 64) if half == 0 else (lane >= 64)


def fill_rows(dst, own, far):
    for h in range(8):
        for half in range(2):
            dst[h, :, 128 * half : 128 * (half + 1)] = own[2 * h + half]
            for j in range(3):
                lo = 256 * (j + 1) + 128 * half
                dst[h, :, lo : lo + 128] = far[2 * h + half, j]


def heads(body, lo=0, hi=4):
    def pair(p, carry):
        for half in range(2):
            body(p, half, 2 * p + half)
        return carry

    lax.fori_loop(lo, hi, pair, 0)


def own_part(ref, p, half):
    return jnp.where(half_mask(half), ref[p, 0:256, :], jnp.zeros((), BF16))


def merge(dst, p, half, value):
    if half == 0:
        dst[p] = value
    else:
        dst[p] = jnp.where(half_mask(0), dst[p], value)


def join(ref):
    return jnp.concatenate([ref[p] for p in range(4)], axis=1)


def turn_rows(ref):
    return jnp.transpose(join(ref), (1, 0))


def weight_term(m, left, right_of, terms):
    first = half_mask(0)
    for q in range(2):
        full = nn(left, jnp.concatenate([right_of(2 * q), right_of(2 * q + 1)], axis=1))
        for r in range(2):
            low = full[:256, 128 * r : 128 * (r + 1)]
            high = full[256:, 128 * r : 128 * (r + 1)]
            even = jnp.where(first, low, pltpu.roll(high, 64, 1))
            odd = jnp.where(first, pltpu.roll(low, 64, 1), high)
            terms[m, 0, 2 * q + r] = even.astype(BF16).reshape(4, 64, 128)
            terms[m, 1, 2 * q + r] = odd.astype(BF16).reshape(4, 64, 128)


def core_copy(m, terms, got_core, send_sem, recv_sem):
    x, y, z, core = position()
    return pltpu.make_async_remote_copy(
        src_ref=terms.at[m, 1 - core],
        dst_ref=got_core.at[m],
        send_sem=send_sem,
        recv_sem=recv_sem,
        device_id=place(x, y, z, 1 - core),
        device_id_type=MESH,
    )


def to_plane(m, terms, got_core, sum_core, got_plane, core_send, core_recv, send_sem, recv_sem):
    x, y, z, core = position()
    core_copy(m, terms, got_core, core_send, core_recv).wait()
    for p in range(4):
        sum_core[m, p] = (terms[m, core, p].astype(F32) + got_core[m, p].astype(F32)).astype(BF16)

    def step(i, carry):
        tx = lax.rem(x + lax.rem(i, 4), 4)
        ty = lax.rem(y + lax.div(i, 4), 4)
        pltpu.make_async_remote_copy(
            src_ref=sum_core.at[m, ty, tx],
            dst_ref=got_plane.at[m, i],
            send_sem=send_sem,
            recv_sem=recv_sem,
            device_id=place(tx, ty, z, core),
            device_id_type=MESH,
        ).start()
        return carry

    lax.fori_loop(1, 16, step, 0)


def to_line(m, sum_core, got_plane, sum_plane, got_line, plane_sem, send_sem, recv_sem):
    x, y, z, core = position()
    drain(got_plane.at[m, pl.ds(1, 15)], plane_sem)

    total = sum_core[m, y, x].astype(F32)
    for i in range(1, 16):
        total = total + got_plane[m, i].astype(F32)
    sum_plane[m] = total.astype(BF16)
    for i in range(2):
        tz = 2 * m + i

        @pl.when(z != tz)
        def _():
            pltpu.make_async_remote_copy(
                src_ref=sum_plane.at[m],
                dst_ref=got_line.at[z],
                send_sem=send_sem,
                recv_sem=recv_sem,
                device_id=place(x, y, tz, core),
                device_id_type=MESH,
            ).start()

        @pl.when(z == tz)
        def _():
            pltpu.make_async_copy(sum_plane.at[m], got_line.at[z], recv_sem).start()


def whole_kernel(partners_ref, x_in, g_in, lse_in, wq_in, wk_in, wv_in, wo_in, nodes, result,
                 x, g, lse, wq, wk, wv, wo, load,
                 cut_x, cut_g, cut_l, held_x, held_g, held_l, held_d, pick_x, pick_g, pick_l, pick_d,
                 far_x, far_g, far_l, far_d,
                 q_all, k_all, v_all, d_all, prob, grad_prob, prob_t, grad_prob_t,
                 part_out, out, grad_q, grad_k, grad_v, part_v, deltas,
                 lse_cols, delta_cols, lse_rows, delta_rows,
                 terms, got_core, sum_core, got_plane, sum_plane, got_line,
                 second, late, send, recv, core_send, core_recv, plane_send, plane_recv):
    gx = lax.axis_index("gx")
    gy = lax.axis_index("gy")
    zpos = lax.div(gx, 4) + 2 * lax.div(gy, 8)
    core = lax.rem(gy, 2)
    first, rest = rendezvous(pltpu.get_barrier_semaphore(), second)
    loads = [
        pltpu.make_async_copy(src, dst, load.at[k])
        for k, (src, dst) in enumerate(
            zip((x_in, g_in, lse_in, wq_in, wk_in, wv_in, wo_in), (x, g, lse, wq, wk, wv, wo))
        )
    ]
    for copy in loads:
        copy.start()
    first()
    for copy in loads[:3]:
        copy.wait()
    for c in range(4):
        cut_x[32 * c : 32 * (c + 1)] = x[:, 128 * c : 128 * (c + 1)].reshape(32, 8, 128)
        cut_g[32 * c : 32 * (c + 1)] = g[:, 128 * c : 128 * (c + 1)].reshape(32, 8, 128)
    for h in range(8):
        for half in range(2):
            cut_l[2 * h + half] = lse[h : h + 1, 128 * half : 128 * (half + 1)]
    rest()
    spread(lambda tx, b, k: cut_x.at[piece_of(tx, b, k)], held_x, gx, gy, send.at[0], recv.at[0])
    for copy in loads[3:]:
        copy.wait()
    own = pl.ds(0, 256)
    project(wq, x[...], q_all, own, scale=0.125)
    project(wk, x[...], k_all, own)
    project(wv, x[...], v_all, own)
    project(wo, g[...], d_all, own, transposed=True)
    turned = jnp.transpose(lse[...], (1, 0))
    for h in range(8):
        lse_cols[h] = turned[:, h : h + 1]

    group = lax.div(gy, 8)
    inner = lax.rem(gy, 8)
    slot = piece_of(gx, group, inner)
    small_slot = small_of(gx, group, inner)
    def own_forward(p, half, h):
        score = nt(own_part(q_all, p, half), k_all[p, 0:256, :])
        prob[h, :, 0:256] = jnp.exp(jnp.minimum(score - lse_cols[h], 0.0))
        part_out[h] = nn(prob[h, :, 0:256].astype(BF16), v_all[p, 0:256, :])
        grad_prob[h, :, 0:256] = nt(own_part(d_all, p, half), v_all[p, 0:256, :])

    heads(own_forward)

    def own_reverse(p, half, h):
        score = nt(own_part(k_all, p, half), q_all[p, 0:256, :])
        row = jnp.concatenate([cut_l[2 * h], cut_l[2 * h + 1]], axis=1)
        prob_t[h] = jnp.exp(jnp.minimum(score - row, 0.0))
        part_v[h] = nn(prob_t[h].astype(BF16), d_all[p, 0:256, :])
        grad_prob_t[h] = nt(own_part(v_all, p, half), d_all[p, 0:256, :])

    heads(own_reverse)

    spread(lambda tx, b, k: cut_g.at[piece_of(tx, b, k)], held_g, gx, gy, send.at[1], recv.at[1], 0, SPLIT)
    spread_small(cut_l, held_l, gx, gy, send.at[2], recv.at[2])
    drain(held_x, recv.at[0])
    choose_wide(partners_ref, held_x, pick_x)
    deliver_wide(slot, pick_x, far_x, send.at[3], recv.at[3], late.at[0])

    drain(far_x.at[pl.ds(0, 8 * EARLY)], recv.at[3])
    spread(lambda tx, b, k: cut_g.at[piece_of(tx, b, k)], held_g, gx, gy, send.at[1], recv.at[1], SPLIT, 32)
    holder = lax.rem(group, 2) == 0

    @pl.when(holder)
    def _():
        pass_small(partners_ref, held_l, pick_l, far_l, small_slot, send.at[5], recv.at[2], recv.at[5])

    drain(far_x.at[pl.ds(0, 128 - 8 * EARLY)], late.at[0])
    for j in range(3):
        rows = pl.ds(256 * (j + 1), 256)
        src = unpack(far_x, j)
        project(wk, src, k_all, rows)
        project(wv, src, v_all, rows)
        project(wq, src, q_all, rows, scale=0.125)

    def forward(p, half, h):
        score = nt(own_part(q_all, p, half), k_all[p, 256:, :])
        prob[h, :, 256:] = jnp.exp(jnp.minimum(score - lse_cols[h], 0.0))
        low = (part_out[h] + nn(prob[h, :, 256:].astype(BF16), v_all[p, 256:, :])).astype(BF16)
        d_own = own_part(d_all, p, half)
        grad_prob[h, :, 256:] = nt(d_own, v_all[p, 256:, :])
        delta = jnp.sum(d_own.astype(F32) * low.astype(F32), axis=1, keepdims=True)
        delta_cols[h] = delta
        merge(out, p, half, low)

    heads(forward)
    lane = lax.broadcasted_iota(jnp.int32, (256, 128), 1)
    flat = jnp.zeros((256, 128), F32)
    for h in range(8):
        flat = jnp.where(lane == h, delta_cols[h], flat)
    turned = jnp.transpose(flat, (1, 0))
    for h in range(8):
        for half in range(2):
            deltas[2 * h + half] = turned[h : h + 1, 128 * half : 128 * (half + 1)]
    spread(lambda tx, b, k: deltas.at[small_of(tx, b, k)], held_d, gx, gy, send.at[6], recv.at[6])
    drain(held_g, recv.at[1])
    choose_wide(partners_ref, held_g, pick_g)
    deliver_wide(slot, pick_g, far_g, send.at[4], recv.at[4], late.at[1])
    def forward_grad(p, half, h):
        grad_score = (prob[h] * (grad_prob[h] - delta_cols[h])).astype(BF16)
        merge(grad_q, p, half, (nn(grad_score, k_all[p]) * 0.125).astype(BF16))

    heads(forward_grad)

    x_turned = jnp.transpose(x[...], (1, 0))
    weight_term(0, x_turned, lambda p: grad_q[p], terms)
    core_copy(0, terms, got_core, core_send.at[0], core_recv.at[0]).start()
    out_turned = turn_rows(out)
    weight_term(3, out_turned, lambda p: g[:, 128 * p : 128 * (p + 1)], terms)
    core_copy(3, terms, got_core, core_send.at[3], core_recv.at[3]).start()

    drain(far_l, recv.at[5])
    fill_rows(lse_rows, cut_l, far_l)
    def reverse_prob(p, half, h):
        score = nt(own_part(k_all, p, half), q_all[p, 256:, :])
        prob[h, :, 256:] = jnp.exp(jnp.minimum(score - lse_rows[h, :, 256:], 0.0))

    heads(reverse_prob)

    drain(held_d, recv.at[6])
    choose(cube_target, 16, partners_ref, held_d, pick_d)
    deliver(cube_target, 16, 0, small_slot, pick_d, far_d, send.at[7], recv.at[7])

    to_plane(0, terms, got_core, sum_core, got_plane, core_send.at[0], core_recv.at[0], plane_send.at[0], plane_recv.at[0])
    to_plane(3, terms, got_core, sum_core, got_plane, core_send.at[3], core_recv.at[3], plane_send.at[3], plane_recv.at[3])

    drain(far_g.at[pl.ds(0, 8 * EARLY)], recv.at[4])
    drain(far_g.at[pl.ds(0, 128 - 8 * EARLY)], late.at[1])
    for j in range(3):
        project(wo, unpack(far_g, j), d_all, pl.ds(256 * (j + 1), 256), transposed=True)

    def reverse_value(p, half, h):
        low = (part_v[h] + nn(prob[h, :, 256:].astype(BF16), d_all[p, 256:, :])).astype(BF16)
        merge(grad_v, p, half, low)

    heads(reverse_value)
    weight_term(2, x_turned, lambda p: grad_v[p], terms)
    core_copy(2, terms, got_core, core_send.at[2], core_recv.at[2]).start()

    def reverse_prob_grad(p, half, h):
        grad_prob[h, :, 256:] = nt(own_part(v_all, p, half), d_all[p, 256:, :])

    heads(reverse_prob_grad)
    to_plane(2, terms, got_core, sum_core, got_plane, core_send.at[2], core_recv.at[2], plane_send.at[2], plane_recv.at[2])
    drain(far_d, recv.at[7])
    fill_rows(delta_rows, deltas, far_d)
    def reverse_grad(p, half, h):
        near = (prob_t[h] * (grad_prob_t[h] - delta_rows[h, :, 0:256])).astype(BF16)
        far = (prob[h, :, 256:] * (grad_prob[h, :, 256:] - delta_rows[h, :, 256:])).astype(BF16)
        both = nn(near, q_all[p, 0:256, :]) + nn(far, q_all[p, 256:, :])
        merge(grad_k, p, half, both.astype(BF16))

    heads(reverse_grad)
    weight_term(1, x_turned, lambda p: grad_k[p], terms)
    core_copy(1, terms, got_core, core_send.at[1], core_recv.at[1]).start()

    nodes[...] = nt(join(grad_q), wq[...]) + nt(join(grad_v), wv[...]) + nt(join(grad_k), wk[...])
    to_plane(1, terms, got_core, sum_core, got_plane, core_send.at[1], core_recv.at[1], plane_send.at[1], plane_recv.at[1])
    for m in (0, 3, 2):
        to_line(m, sum_core, got_plane, sum_plane, got_line, plane_recv.at[m], send.at[8], recv.at[8])
    to_line(1, sum_core, got_plane, sum_plane, got_line, plane_recv.at[1], send.at[8], recv.at[8])
    drain(got_line, recv.at[8])
    acc = got_line[0].astype(F32)
    for i in range(1, 8):
        acc = acc + got_line[i].astype(F32)
    result[...] = jnp.where(lax.rem(zpos, 2) == 0, acc[:, :64], acc[:, 64:])

    drain(held_d.at[pl.ds(0, DEVICES - 1)], send.at[6])
    drain(far_d.at[pl.ds(0, 15)], send.at[7])
    for k, ref in enumerate((held_x, held_g)):
        drain(ref.at[pl.ds(0, DEVICES - 1)], send.at[k])
    for k, ref in enumerate((far_x, far_g)):
        drain(ref.at[pl.ds(0, PIECES - 1)], send.at[3 + k])

    @pl.when(holder)
    def _():
        drain(held_l.at[pl.ds(0, 127)], send.at[2])
        drain(pick_l.at[pl.ds(0, 31)], send.at[5])

    @pl.when(jnp.logical_not(holder))
    def _():
        drain(held_l.at[pl.ds(0, 128)], send.at[2])

    for m in range(4):
        drain(got_plane.at[m, pl.ds(1, 15)], plane_send.at[m])
    drain(got_line.at[pl.ds(0, 7)], send.at[8])


def vmem(count):
    return [pl.BlockSpec(memory_space=pltpu.VMEM)] * count


def sds(shape, kind):
    return jax.ShapeDtypeStruct(shape, kind)


def params(cid=None):
    if cid is None:
        return pltpu.CompilerParams(vmem_limit_bytes=LIMIT)
    return pltpu.CompilerParams(vmem_limit_bytes=LIMIT, collective_id=cid, has_side_effects=True)


def on_device(x, g, lse, wq, wk, wv, wo, partners):
    smem = pl.BlockSpec(memory_space=pltpu.SMEM)
    dma = pltpu.SemaphoreType.DMA
    regular = pltpu.SemaphoreType.REGULAR
    wide = pltpu.VMEM((PIECES, 3, 8, 128), BF16)
    small = pltpu.VMEM((16, 3, 1, 128), F32)
    held = pltpu.VMEM((DEVICES, 8, 128), BF16)
    held_small = pltpu.VMEM((DEVICES, 1, 128), F32)
    pick_small = pltpu.VMEM((32, 3, 1, 128), F32)
    cut = pltpu.VMEM((PIECES, 8, 128), BF16)
    cut_small = pltpu.VMEM((16, 1, 128), F32)
    split = pltpu.VMEM((4, 1024, 128), BF16)
    square = pltpu.VMEM((8, 256, 1024), F32)
    tile = pltpu.VMEM((8, 256, 256), F32)
    part = pltpu.VMEM((8, 256, 128), F32)
    joined = pltpu.VMEM((4, 256, 128), BF16)
    column = pltpu.VMEM((8, 256, 1), F32)
    row = pltpu.VMEM((8, 1, 1024), F32)
    rows = pltpu.VMEM((256, 512), BF16)
    weight = pltpu.VMEM((512, 512), BF16)
    tiles = pltpu.VMEM((4, 4, 4, 64, 128), BF16)
    nodes, result = pl.pallas_call(
        whole_kernel,
        out_shape=(sds((256, 512), F32), sds((64, 64), F32)),
        in_specs=[smem] + [pl.BlockSpec(memory_space=pltpu.HBM)] * 7,
        out_specs=tuple(vmem(2)),
        scratch_shapes=[
            rows, rows, pltpu.VMEM((8, 256), F32), weight, weight, weight, weight, dma((7,)),
            cut, cut, cut_small, held, held, held_small, held_small, wide, wide, pick_small, small,
            wide, wide, small, small,
            split, split, split, split, square, square, tile, tile,
            part, joined, joined, joined, joined, part, cut_small,
            column, column, row, row,
            pltpu.VMEM((4, 2, 4, 4, 64, 128), BF16), tiles, tiles, pltpu.VMEM((4, 16, 64, 128), BF16),
            pltpu.VMEM((4, 64, 128), BF16), pltpu.VMEM((8, 64, 128), BF16),
            regular, dma((2,)), dma((9,)), dma((9,)), dma((4,)), dma((4,)), dma((4,)), dma((4,)),
        ],
        compiler_params=params(0),
        name="whole",
    )(*(pltpu.with_memory_space_constraint(a, pltpu.HBM) for a in (partners.T, x, g, lse, wq, wk, wv, wo)))
    return nodes.astype(BF16), result


def solution(mesh):
    return jax.shard_map(
        on_device,
        mesh=mesh,
        in_specs=(
            P(("gx", "gy"), None),
            P(("gx", "gy"), None),
            P(None, ("gx", "gy")),
            P(),
            P(),
            P(),
            P(),
            P(),
        ),
        out_specs=(P(("gx", "gy"), None), P("gx", "gy")),
        check_vma=False,
    )
```

```python
import functools

import jax
import jax.numpy as jnp
from jax import lax
from jax.experimental import pallas as pl
from jax.experimental.pallas import tpu as pltpu
from jax.sharding import PartitionSpec as P

MESH = pl.DeviceIdType.MESH
F32 = jnp.float32
BF16 = jnp.bfloat16
DEVICES = 256
PIECES = 128
SPLIT = 16
EARLY = 10
LIMIT = 50 * 1024 * 1024


def nt(a, b):
    return lax.dot_general(a, b, (((1,), (1,)), ((), ())), preferred_element_type=F32)


def nn(a, b):
    return lax.dot_general(a, b, (((1,), (0,)), ((), ())), preferred_element_type=F32)


def position():
    gx = lax.axis_index("gx")
    gy = lax.axis_index("gy")
    x = lax.rem(gx, 4)
    y = lax.rem(lax.div(gy, 2), 4)
    z = lax.div(gx, 4) + 2 * lax.div(gy, 8)
    core = lax.rem(gy, 2)
    return x, y, z, core


def place(x, y, z, core):
    return lax.rem(z, 2) * 4 + x, (lax.div(z, 2) * 4 + y) * 2 + core


def rendezvous(barrier, second):
    x, y, z, core = position()

    def signal(sem, peer):
        pl.semaphore_signal(sem, inc=1, device_id=peer, device_id_type=MESH)

    def line(sem):
        for i in (4, 3, 5, 2, 6, 1, 7):
            signal(sem, place(x, y, lax.rem(z + i, 8), core))

    def first():
        line(barrier)
        for dy in (2, 1, 3, 0):
            for dx in (2, 1, 3, 0):
                for dc in (1, 0):
                    if dx or dy or dc:
                        signal(barrier, place(lax.rem(x + dx, 4), lax.rem(y + dy, 4), z, lax.rem(core + dc, 2)))

    def rest():
        pl.semaphore_wait(barrier, 38)
        line(second)
        pl.semaphore_wait(second, 7)

    return first, rest


def spread(src_of, dst, gx, gy, send_sem, recv_sem, lo=0, hi=32):
    me = gx * 32 + gy
    group = lax.div(gy, 8)
    inner = lax.rem(gy, 8)

    def send(tx, b, k):
        pltpu.make_async_remote_copy(
            src_ref=src_of(tx, b, k),
            dst_ref=dst.at[me],
            send_sem=send_sem,
            recv_sem=recv_sem,
            device_id=(tx, 8 * b + k),
            device_id_type=MESH,
        ).start()

    def octet(i, carry):
        tx = lax.rem(gx + lax.div(i, 4), 8)
        b = lax.rem(group + lax.rem(i, 4), 4)
        for k in range(8):
            send(tx, b, k)
        return carry

    lax.fori_loop(max(lo, 1), hi, octet, 0)
    if lo == 0:
        for k in range(1, 8):
            send(gx, group, lax.rem(inner + k, 8))
        pltpu.make_async_copy(src_of(gx, group, inner), dst.at[me], recv_sem).start()


def drain(ref, sem):
    pltpu.make_async_copy(ref, ref, sem).wait()


def piece_of(tx, b, k):
    return tx * 16 + 8 * lax.rem(b, 2) + k


def small_of(tx, b, k):
    return (lax.div(tx, 4) * 2 + lax.rem(tx, 2)) * 4 + (k % 4 if isinstance(k, int) else lax.rem(k, 4))


def wide_octet(a):
    x, y, z, core = position()
    tz = lax.rem(z + lax.rem(lax.div(a, 4) + 1 + core, 4) + 7 - core, 8)
    tx = lax.rem(tz, 2) * 4 + lax.rem(x + lax.rem(a, 4), 4)
    return tx, lax.div(tz, 2)


def choose_wide(partners_ref, held, chosen):
    def octet(a, carry):
        tx, b = wide_octet(a)
        block = tx * 32 + 8 * b
        for k in range(8):
            for j in range(3):
                chosen[8 * a + k, j] = held[partners_ref[j, block + k]]
        return carry

    lax.fori_loop(0, 16, octet, 0)


def deliver_wide(slot, chosen, dst, send_sem, early_sem, late_sem):
    inner = lax.rem(lax.axis_index("gy"), 8)

    def send(a, tx, b, k, recv_sem):
        pltpu.make_async_remote_copy(
            src_ref=chosen.at[8 * a + k],
            dst_ref=dst.at[slot],
            send_sem=send_sem,
            recv_sem=recv_sem,
            device_id=(tx, 8 * b + k),
            device_id_type=MESH,
        ).start()

    def octets(lo, hi, recv_sem):
        def octet(a, carry):
            tx, b = wide_octet(a)
            for k in range(8):
                send(a, tx, b, k, recv_sem)
            return carry

        lax.fori_loop(lo, hi, octet, 0)

    octets(1, EARLY, early_sem)
    tx, b = wide_octet(0)
    for k in range(1, 8):
        send(0, tx, b, lax.rem(inner + k, 8), early_sem)
    pltpu.make_async_copy(chosen.at[inner], dst.at[slot], early_sem).start()
    octets(EARLY, 16, late_sem)


def small_target(index):
    x, y, z, core = position()
    tx = lax.div(x, 2) * 2 + lax.rem(x + lax.rem(index, 2), 2)
    ty = lax.div(y, 2) * 2 + lax.rem(y + lax.rem(lax.div(index, 2), 2), 2)
    tz = lax.div(z, 4) * 4 + lax.rem(z + lax.rem(lax.div(index, 4), 4), 4)
    tc = lax.rem(core + lax.div(index, 16), 2)
    return place(tx, ty, tz, tc)


def spread_small(src, dst, gx, gy, send_sem, recv_sem):
    me = gx * 32 + gy
    group = lax.div(gy, 8)
    inner = lax.rem(gy, 8)

    def send(tx, b, k):
        pltpu.make_async_remote_copy(
            src_ref=src.at[small_of(tx, b, k)],
            dst_ref=dst.at[me],
            send_sem=send_sem,
            recv_sem=recv_sem,
            device_id=(tx, 8 * b + k),
            device_id_type=MESH,
        ).start()

    def octet(i, carry):
        tx = lax.rem(gx + lax.div(i, 2), 8)
        b = 2 * lax.rem(i, 2)
        for k in range(8):
            send(tx, b, k)
        return carry

    lax.fori_loop(2, 16, octet, 0)
    for b in (0, 2):

        @pl.when(group != b)
        def _():
            for k in range(8):
                send(gx, b, k)

        @pl.when(group == b)
        def _():
            for k in range(1, 8):
                send(gx, b, lax.rem(inner + k, 8))
            pltpu.make_async_copy(src.at[small_of(gx, b, inner)], dst.at[me], recv_sem).start()


def pass_small(partners_ref, held, chosen, dst, slot, send_sem, held_sem, recv_sem):
    drain(held, held_sem)

    def pick(index, carry):
        tx, ty = small_target(index)
        block = tx * 32 + ty
        for j in range(3):
            chosen[index, j] = held[partners_ref[j, block]]
        return carry

    lax.fori_loop(0, 32, pick, 0)

    def send(index, carry):
        tx, ty = small_target(index)
        pltpu.make_async_remote_copy(
            src_ref=chosen.at[index],
            dst_ref=dst.at[slot],
            send_sem=send_sem,
            recv_sem=recv_sem,
            device_id=(tx, ty),
            device_id_type=MESH,
        ).start()
        return carry

    lax.fori_loop(1, 32, send, 0)
    pltpu.make_async_copy(chosen.at[0], dst.at[slot], recv_sem).start()


def cube_target(index):
    x, y, z, core = position()
    tx = lax.div(x, 2) * 2 + lax.rem(x + lax.rem(index, 2), 2)
    ty = lax.div(y, 2) * 2 + lax.rem(y + lax.rem(lax.div(index, 2), 2), 2)
    tz = lax.div(z, 2) * 2 + lax.rem(z + lax.rem(lax.div(index, 4), 2), 2)
    tc = lax.rem(core + lax.div(index, 8), 2)
    return place(tx, ty, tz, tc)


def choose(target, count, partners_ref, held, chosen):
    def pick(index, carry):
        tx, ty = target(index)
        block = tx * 32 + ty
        for j in range(3):
            chosen[index, j] = held[partners_ref[j, block]]
        return carry

    lax.fori_loop(0, count, pick, 0)


def deliver(target, count, self_index, slot, chosen, dst, send_sem, recv_sem):
    def send(index, carry):
        tx, ty = target(index)
        pltpu.make_async_remote_copy(
            src_ref=chosen.at[index],
            dst_ref=dst.at[slot],
            send_sem=send_sem,
            recv_sem=recv_sem,
            device_id=(tx, ty),
            device_id_type=MESH,
        ).start()
        return carry

    lax.fori_loop(0, self_index, send, 0)
    lax.fori_loop(self_index + 1, count, send, 0)
    pltpu.make_async_copy(chosen.at[self_index], dst.at[slot], recv_sem).start()


def project(w, src, dst, rows, scale=None, transposed=False):
    full = nt(src, w[...]) if transposed else nn(src, w[...])
    low = full.astype(BF16)
    if scale is not None:
        low = low * jnp.asarray(scale, BF16)
    for p in range(4):
        dst[p, rows, :] = low[:, 128 * p : 128 * (p + 1)]


def unpack(far, j):
    return jnp.concatenate([far[32 * c : 32 * (c + 1), j].reshape(256, 128) for c in range(4)], axis=1)


def half_mask(half):
    lane = lax.broadcasted_iota(jnp.int32, (1, 128), 1)
    return (lane < 64) if half == 0 else (lane >= 64)


def fill_rows(dst, own, far):
    for h in range(8):
        for half in range(2):
            dst[h, :, 128 * half : 128 * (half + 1)] = own[2 * h + half]
            for j in range(3):
                lo = 256 * (j + 1) + 128 * half
                dst[h, :, lo : lo + 128] = far[2 * h + half, j]


def heads(body, lo=0, hi=4):
    def pair(p, carry):
        for half in range(2):
            body(p, half, 2 * p + half)
        return carry

    lax.fori_loop(lo, hi, pair, 0)


def own_part(ref, p, half):
    return jnp.where(half_mask(half), ref[p, 0:256, :], jnp.zeros((), BF16))


def merge(dst, p, half, value):
    if half == 0:
        dst[p] = value
    else:
        dst[p] = jnp.where(half_mask(0), dst[p], value)


def join(ref):
    return jnp.concatenate([ref[p] for p in range(4)], axis=1)


def turn_rows(ref):
    return jnp.transpose(join(ref), (1, 0))


def weight_term(m, left, right_of, terms):
    first = half_mask(0)
    for q in range(2):
        full = nn(left, jnp.concatenate([right_of(2 * q), right_of(2 * q + 1)], axis=1))
        for r in range(2):
            low = full[:256, 128 * r : 128 * (r + 1)]
            high = full[256:, 128 * r : 128 * (r + 1)]
            even = jnp.where(first, low, pltpu.roll(high, 64, 1))
            odd = jnp.where(first, pltpu.roll(low, 64, 1), high)
            terms[m, 0, 2 * q + r] = even.astype(BF16).reshape(4, 64, 128)
            terms[m, 1, 2 * q + r] = odd.astype(BF16).reshape(4, 64, 128)


def core_copy(m, terms, got_core, send_sem, recv_sem):
    x, y, z, core = position()
    return pltpu.make_async_remote_copy(
        src_ref=terms.at[m, 1 - core],
        dst_ref=got_core.at[m],
        send_sem=send_sem,
        recv_sem=recv_sem,
        device_id=place(x, y, z, 1 - core),
        device_id_type=MESH,
    )


def to_plane(m, terms, got_core, sum_core, got_plane, core_send, core_recv, send_sem, recv_sem):
    x, y, z, core = position()
    core_copy(m, terms, got_core, core_send, core_recv).wait()
    for p in range(4):
        sum_core[m, p] = (terms[m, core, p].astype(F32) + got_core[m, p].astype(F32)).astype(BF16)

    def step(i, carry):
        tx = lax.rem(x + lax.rem(i, 4), 4)
        ty = lax.rem(y + lax.div(i, 4), 4)
        pltpu.make_async_remote_copy(
            src_ref=sum_core.at[m, ty, tx],
            dst_ref=got_plane.at[m, i],
            send_sem=send_sem,
            recv_sem=recv_sem,
            device_id=place(tx, ty, z, core),
            device_id_type=MESH,
        ).start()
        return carry

    lax.fori_loop(1, 16, step, 0)


def to_line(m, sum_core, got_plane, sum_plane, got_line, plane_sem, send_sem, recv_sem):
    x, y, z, core = position()
    drain(got_plane.at[m, pl.ds(1, 15)], plane_sem)

    total = sum_core[m, y, x].astype(F32)
    for i in range(1, 16):
        total = total + got_plane[m, i].astype(F32)
    sum_plane[m] = total.astype(BF16)
    for i in range(2):
        tz = 2 * m + i

        @pl.when(z != tz)
        def _():
            pltpu.make_async_remote_copy(
                src_ref=sum_plane.at[m],
                dst_ref=got_line.at[z],
                send_sem=send_sem,
                recv_sem=recv_sem,
                device_id=place(x, y, tz, core),
                device_id_type=MESH,
            ).start()

        @pl.when(z == tz)
        def _():
            pltpu.make_async_copy(sum_plane.at[m], got_line.at[z], recv_sem).start()


def whole_kernel(partners_ref, x_in, g_in, lse_in, wq_in, wk_in, wv_in, wo_in, nodes, result,
                 x, g, lse, wq, wk, wv, wo, load,
                 cut_x, cut_g, cut_l, held_x, held_g, held_l, held_d, pick_x, pick_g, pick_l, pick_d,
                 far_x, far_g, far_l, far_d,
                 q_all, k_all, v_all, d_all, prob, grad_prob, prob_t, grad_prob_t,
                 part_out, out, grad_q, grad_k, grad_v, part_v, deltas,
                 lse_cols, delta_cols, lse_rows, delta_rows,
                 terms, got_core, sum_core, got_plane, sum_plane, got_line,
                 second, late, send, recv, core_send, core_recv, plane_send, plane_recv):
    gx = lax.axis_index("gx")
    gy = lax.axis_index("gy")
    zpos = lax.div(gx, 4) + 2 * lax.div(gy, 8)
    core = lax.rem(gy, 2)
    first, rest = rendezvous(pltpu.get_barrier_semaphore(), second)
    loads = [
        pltpu.make_async_copy(src, dst, load.at[k])
        for k, (src, dst) in enumerate(
            zip((x_in, g_in, lse_in, wq_in, wk_in, wv_in, wo_in), (x, g, lse, wq, wk, wv, wo))
        )
    ]
    for copy in loads:
        copy.start()
    first()
    for copy in loads[:3]:
        copy.wait()
    for c in range(4):
        cut_x[32 * c : 32 * (c + 1)] = x[:, 128 * c : 128 * (c + 1)].reshape(32, 8, 128)
        cut_g[32 * c : 32 * (c + 1)] = g[:, 128 * c : 128 * (c + 1)].reshape(32, 8, 128)
    for h in range(8):
        for half in range(2):
            cut_l[2 * h + half] = lse[h : h + 1, 128 * half : 128 * (half + 1)]
    rest()
    spread(lambda tx, b, k: cut_x.at[piece_of(tx, b, k)], held_x, gx, gy, send.at[0], recv.at[0])
    for copy in loads[3:]:
        copy.wait()
    own = pl.ds(0, 256)
    project(wq, x[...], q_all, own, scale=0.125)
    project(wk, x[...], k_all, own)
    project(wv, x[...], v_all, own)
    project(wo, g[...], d_all, own, transposed=True)
    turned = jnp.transpose(lse[...], (1, 0))
    for h in range(8):
        lse_cols[h] = turned[:, h : h + 1]

    group = lax.div(gy, 8)
    inner = lax.rem(gy, 8)
    slot = piece_of(gx, group, inner)
    small_slot = small_of(gx, group, inner)
    def own_forward(p, half, h):
        score = nt(own_part(q_all, p, half), k_all[p, 0:256, :])
        prob[h, :, 0:256] = jnp.exp(jnp.minimum(score - lse_cols[h], 0.0))
        part_out[h] = nn(prob[h, :, 0:256].astype(BF16), v_all[p, 0:256, :])
        grad_prob[h, :, 0:256] = nt(own_part(d_all, p, half), v_all[p, 0:256, :])

    heads(own_forward)

    def own_reverse(p, half, h):
        score = nt(own_part(k_all, p, half), q_all[p, 0:256, :])
        row = jnp.concatenate([cut_l[2 * h], cut_l[2 * h + 1]], axis=1)
        prob_t[h] = jnp.exp(jnp.minimum(score - row, 0.0))
        part_v[h] = nn(prob_t[h].astype(BF16), d_all[p, 0:256, :])
        grad_prob_t[h] = nt(own_part(v_all, p, half), d_all[p, 0:256, :])

    heads(own_reverse)

    spread(lambda tx, b, k: cut_g.at[piece_of(tx, b, k)], held_g, gx, gy, send.at[1], recv.at[1], 0, SPLIT)
    spread_small(cut_l, held_l, gx, gy, send.at[2], recv.at[2])
    drain(held_x, recv.at[0])
    choose_wide(partners_ref, held_x, pick_x)
    deliver_wide(slot, pick_x, far_x, send.at[3], recv.at[3], late.at[0])

    drain(far_x.at[pl.ds(0, 8 * EARLY)], recv.at[3])
    spread(lambda tx, b, k: cut_g.at[piece_of(tx, b, k)], held_g, gx, gy, send.at[1], recv.at[1], SPLIT, 32)
    holder = lax.rem(group, 2) == 0

    @pl.when(holder)
    def _():
        pass_small(partners_ref, held_l, pick_l, far_l, small_slot, send.at[5], recv.at[2], recv.at[5])

    drain(far_x.at[pl.ds(0, 128 - 8 * EARLY)], late.at[0])
    for j in range(3):
        rows = pl.ds(256 * (j + 1), 256)
        src = unpack(far_x, j)
        project(wk, src, k_all, rows)
        project(wv, src, v_all, rows)
        project(wq, src, q_all, rows, scale=0.125)

    def forward(p, half, h):
        score = nt(own_part(q_all, p, half), k_all[p, 256:, :])
        prob[h, :, 256:] = jnp.exp(jnp.minimum(score - lse_cols[h], 0.0))
        low = (part_out[h] + nn(prob[h, :, 256:].astype(BF16), v_all[p, 256:, :])).astype(BF16)
        d_own = own_part(d_all, p, half)
        grad_prob[h, :, 256:] = nt(d_own, v_all[p, 256:, :])
        delta = jnp.sum(d_own.astype(F32) * low.astype(F32), axis=1, keepdims=True)
        delta_cols[h] = delta
        merge(out, p, half, low)

    heads(forward)
    lane = lax.broadcasted_iota(jnp.int32, (256, 128), 1)
    flat = jnp.zeros((256, 128), F32)
    for h in range(8):
        flat = jnp.where(lane == h, delta_cols[h], flat)
    turned = jnp.transpose(flat, (1, 0))
    for h in range(8):
        for half in range(2):
            deltas[2 * h + half] = turned[h : h + 1, 128 * half : 128 * (half + 1)]
    spread(lambda tx, b, k: deltas.at[small_of(tx, b, k)], held_d, gx, gy, send.at[6], recv.at[6])
    drain(held_g, recv.at[1])
    choose_wide(partners_ref, held_g, pick_g)
    deliver_wide(slot, pick_g, far_g, send.at[4], recv.at[4], late.at[1])
    def forward_grad(p, half, h):
        grad_score = (prob[h] * (grad_prob[h] - delta_cols[h])).astype(BF16)
        merge(grad_q, p, half, (nn(grad_score, k_all[p]) * 0.125).astype(BF16))

    heads(forward_grad)

    x_turned = jnp.transpose(x[...], (1, 0))
    weight_term(0, x_turned, lambda p: grad_q[p], terms)
    core_copy(0, terms, got_core, core_send.at[0], core_recv.at[0]).start()
    out_turned = turn_rows(out)
    weight_term(3, out_turned, lambda p: g[:, 128 * p : 128 * (p + 1)], terms)
    core_copy(3, terms, got_core, core_send.at[3], core_recv.at[3]).start()

    drain(far_l, recv.at[5])
    fill_rows(lse_rows, cut_l, far_l)
    def reverse_prob(p, half, h):
        score = nt(own_part(k_all, p, half), q_all[p, 256:, :])
        prob[h, :, 256:] = jnp.exp(jnp.minimum(score - lse_rows[h, :, 256:], 0.0))

    heads(reverse_prob)

    drain(held_d, recv.at[6])
    choose(cube_target, 16, partners_ref, held_d, pick_d)
    deliver(cube_target, 16, 0, small_slot, pick_d, far_d, send.at[7], recv.at[7])

    to_plane(0, terms, got_core, sum_core, got_plane, core_send.at[0], core_recv.at[0], plane_send.at[0], plane_recv.at[0])
    to_plane(3, terms, got_core, sum_core, got_plane, core_send.at[3], core_recv.at[3], plane_send.at[3], plane_recv.at[3])

    drain(far_g.at[pl.ds(0, 8 * EARLY)], recv.at[4])
    drain(far_g.at[pl.ds(0, 128 - 8 * EARLY)], late.at[1])
    for j in range(3):
        project(wo, unpack(far_g, j), d_all, pl.ds(256 * (j + 1), 256), transposed=True)

    def reverse_value(p, half, h):
        low = (part_v[h] + nn(prob[h, :, 256:].astype(BF16), d_all[p, 256:, :])).astype(BF16)
        merge(grad_v, p, half, low)

    heads(reverse_value)
    weight_term(2, x_turned, lambda p: grad_v[p], terms)
    core_copy(2, terms, got_core, core_send.at[2], core_recv.at[2]).start()

    def reverse_prob_grad(p, half, h):
        grad_prob[h, :, 256:] = nt(own_part(v_all, p, half), d_all[p, 256:, :])

    heads(reverse_prob_grad)
    to_plane(2, terms, got_core, sum_core, got_plane, core_send.at[2], core_recv.at[2], plane_send.at[2], plane_recv.at[2])
    drain(far_d, recv.at[7])
    fill_rows(delta_rows, deltas, far_d)
    def reverse_grad(p, half, h):
        near = (prob_t[h] * (grad_prob_t[h] - delta_rows[h, :, 0:256])).astype(BF16)
        far = (prob[h, :, 256:] * (grad_prob[h, :, 256:] - delta_rows[h, :, 256:])).astype(BF16)
        both = nn(near, q_all[p, 0:256, :]) + nn(far, q_all[p, 256:, :])
        merge(grad_k, p, half, both.astype(BF16))

    heads(reverse_grad)
    weight_term(1, x_turned, lambda p: grad_k[p], terms)
    core_copy(1, terms, got_core, core_send.at[1], core_recv.at[1]).start()

    nodes[...] = nt(join(grad_q), wq[...]) + nt(join(grad_v), wv[...]) + nt(join(grad_k), wk[...])
    to_plane(1, terms, got_core, sum_core, got_plane, core_send.at[1], core_recv.at[1], plane_send.at[1], plane_recv.at[1])
    for m in (0, 3, 2):
        to_line(m, sum_core, got_plane, sum_plane, got_line, plane_recv.at[m], send.at[8], recv.at[8])
    to_line(1, sum_core, got_plane, sum_plane, got_line, plane_recv.at[1], send.at[8], recv.at[8])
    drain(got_line, recv.at[8])
    acc = got_line[0].astype(F32)
    for i in range(1, 8):
        acc = acc + got_line[i].astype(F32)
    result[...] = jnp.where(lax.rem(zpos, 2) == 0, acc[:, :64], acc[:, 64:])

    drain(held_d.at[pl.ds(0, DEVICES - 1)], send.at[6])
    drain(far_d.at[pl.ds(0, 15)], send.at[7])
    for k, ref in enumerate((held_x, held_g)):
        drain(ref.at[pl.ds(0, DEVICES - 1)], send.at[k])
    for k, ref in enumerate((far_x, far_g)):
        drain(ref.at[pl.ds(0, PIECES - 1)], send.at[3 + k])

    @pl.when(holder)
    def _():
        drain(held_l.at[pl.ds(0, 127)], send.at[2])
        drain(pick_l.at[pl.ds(0, 31)], send.at[5])

    @pl.when(jnp.logical_not(holder))
    def _():
        drain(held_l.at[pl.ds(0, 128)], send.at[2])

    for m in range(4):
        drain(got_plane.at[m, pl.ds(1, 15)], plane_send.at[m])
    drain(got_line.at[pl.ds(0, 7)], send.at[8])


def vmem(count):
    return [pl.BlockSpec(memory_space=pltpu.VMEM)] * count


def sds(shape, kind):
    return jax.ShapeDtypeStruct(shape, kind)


def params(cid=None):
    if cid is None:
        return pltpu.CompilerParams(vmem_limit_bytes=LIMIT)
    return pltpu.CompilerParams(vmem_limit_bytes=LIMIT, collective_id=cid, has_side_effects=True)


def on_device(x, g, lse, wq, wk, wv, wo, partners):
    smem = pl.BlockSpec(memory_space=pltpu.SMEM)
    dma = pltpu.SemaphoreType.DMA
    regular = pltpu.SemaphoreType.REGULAR
    wide = pltpu.VMEM((PIECES, 3, 8, 128), BF16)
    small = pltpu.VMEM((16, 3, 1, 128), F32)
    held = pltpu.VMEM((DEVICES, 8, 128), BF16)
    held_small = pltpu.VMEM((DEVICES, 1, 128), F32)
    pick_small = pltpu.VMEM((32, 3, 1, 128), F32)
    cut = pltpu.VMEM((PIECES, 8, 128), BF16)
    cut_small = pltpu.VMEM((16, 1, 128), F32)
    split = pltpu.VMEM((4, 1024, 128), BF16)
    square = pltpu.VMEM((8, 256, 1024), F32)
    tile = pltpu.VMEM((8, 256, 256), F32)
    part = pltpu.VMEM((8, 256, 128), F32)
    joined = pltpu.VMEM((4, 256, 128), BF16)
    column = pltpu.VMEM((8, 256, 1), F32)
    row = pltpu.VMEM((8, 1, 1024), F32)
    rows = pltpu.VMEM((256, 512), BF16)
    weight = pltpu.VMEM((512, 512), BF16)
    tiles = pltpu.VMEM((4, 4, 4, 64, 128), BF16)
    nodes, result = pl.pallas_call(
        whole_kernel,
        out_shape=(sds((256, 512), F32), sds((64, 64), F32)),
        in_specs=[smem] + [pl.BlockSpec(memory_space=pltpu.HBM)] * 7,
        out_specs=tuple(vmem(2)),
        scratch_shapes=[
            rows, rows, pltpu.VMEM((8, 256), F32), weight, weight, weight, weight, dma((7,)),
            cut, cut, cut_small, held, held, held_small, held_small, wide, wide, pick_small, small,
            wide, wide, small, small,
            split, split, split, split, square, square, tile, tile,
            part, joined, joined, joined, joined, part, cut_small,
            column, column, row, row,
            pltpu.VMEM((4, 2, 4, 4, 64, 128), BF16), tiles, tiles, pltpu.VMEM((4, 16, 64, 128), BF16),
            pltpu.VMEM((4, 64, 128), BF16), pltpu.VMEM((8, 64, 128), BF16),
            regular, dma((2,)), dma((9,)), dma((9,)), dma((4,)), dma((4,)), dma((4,)), dma((4,)),
        ],
        compiler_params=params(0),
        name="whole",
    )(*(pltpu.with_memory_space_constraint(a, pltpu.HBM) for a in (partners.T, x, g, lse, wq, wk, wv, wo)))
    return nodes.astype(BF16), result


def solution(mesh):
    return jax.shard_map(
        on_device,
        mesh=mesh,
        in_specs=(
            P(("gx", "gy"), None),
            P(("gx", "gy"), None),
            P(None, ("gx", "gy")),
            P(),
            P(),
            P(),
            P(),
            P(),
        ),
        out_specs=(P(("gx", "gy"), None), P("gx", "gy")),
        check_vma=False,
    )
```
